32 devices in a mesh: ctx: 8 (over y, x, core), exp: 4 (over z).
Axes of the slice: x: 2, y: 2, z: 4, core: 2. Of those that a mesh axis runs over, the one named last changes fastest.
Arguments:
- conv_input: bfloat16 [1024, 4096], P('ctx', 'exp'), may hold values from -6 to 6
- conv_weight: float32 [4, 4096], P(None, 'exp'), may hold values from -3 to 3
- b_proj: bfloat16 [1024, 128], P('ctx'), may hold values from -0.5 to 0.5
- c_proj: bfloat16 [1024, 128], P('ctx'), may hold values from -0.29882812 to 0.29882812
- log_decay: float32 [64, 1024], P('exp', 'ctx'), may hold values from -1 to 0
- skip_gain: float32 [64], P('exp'), may hold values from 0.5 to 1.5
- grad_in: bfloat16 [1024, 4096], P('ctx', 'exp'), may hold values from -6 to 6
- norm_gain: float32 [4096], replicated, may hold values from 0.1 to 1.9
- expert_ids: int32 [1024, 2], P('ctx'), may hold values from 0 to 3, all different within a row; in each aligned block of 32 rows (0 to 31, 32 to 63, ...) at most 24 rows name the same one
- expert_weights: float32 [1024, 2], P('ctx'), may hold values from 0.1 to 1
- up_weight: bfloat16 [4, 4096, 12288], P('exp', None, 'ctx'), may hold values from -0.09375 to 0.09375
- down_weight: bfloat16 [4, 12288, 4096], P('exp', 'ctx'), may hold values from -0.0546875 to 0.0546875
Outputs:
- moe_out: bfloat16 [1024, 4096], P('ctx', 'exp')
- grad_conv: float32 [1024, 4096], P('ctx', 'exp')
The draws below stay inside these ranges and needn't reach their ends.
Inputs may be any that keep to these rules, and one draw needn't show every extreme that they name: `expert_ids`: each token names 2 different experts; in each aligned block of 32 tokens no expert is named more than 24 times.
All inputs are finite; a program needn't handle non-finite values.
Results may differ from the reference program's by a relative error of at most 0.018.
Values may be sent and summed in bfloat16 or wider, within the bound.
No kernel may reach another device: no remote copies, remote signals or barrier semaphores. Data moves between devices by JAX's collectives and lax.ppermute only.
A program may use at most 128 MiB of HBM per device.

```python
import math
import jax
import jax.numpy as jnp
import numpy as np
from jax import lax

TOK_DEV = 128
HEADS = 64
HEAD_DIM = 64
STATE = 128
CONV = 4
FF = 12288
TOPK = 2
EXPERTS = 4
CHANNELS = 4096
CONTEXT_LENGTH = 1024
MOST = 24
N_CTX = 8
N_EXP = 4


def draw_log_decay(key, part):
    keys = jax.random.split(jax.random.fold_in(key, 11), 5)
    fast_share = 0.5
    fast_heads = jax.random.uniform(keys[0], (HEADS, 1)) < fast_share
    baseline_frequency = jnp.where(fast_heads, 1.0 / 40.0, 0.3 / CONTEXT_LENGTH)
    random_perturbation = jnp.exp(jax.random.uniform(keys[1], (HEADS, CONTEXT_LENGTH), minval=-0.69, maxval=0.69))
    block_factor = jnp.exp(jax.random.uniform(keys[2], (HEADS, N_CTX), minval=-0.35, maxval=0.35))
    complete_block = jnp.repeat(block_factor, TOK_DEV, axis=1)
    marked_locations = jax.random.randint(keys[3], (3,), 0, CONTEXT_LENGTH)
    spike_groups = jnp.any(jnp.arange(CONTEXT_LENGTH)[None, :] == marked_locations[:, None], axis=0)
    loss_values = jnp.log(jax.random.uniform(keys[4], (HEADS, CONTEXT_LENGTH), minval=0.5, maxval=0.8))
    return (-baseline_frequency * random_perturbation * complete_block + jnp.where(spike_groups[None, :], loss_values, 0.0)).astype(jnp.float32)


def levels(own_key, extent, cuts, least, top_value):
    loudness, own = 1.0, jax.random.fold_in(own_key, 6)
    for dim, shards_of in cuts:
        heights = jnp.exp(jax.random.uniform(jax.random.fold_in(own, dim), (shards_of,), jnp.float32, least / len(cuts), top_value / len(cuts)))
        loudness = loudness * jnp.repeat(heights, extent[dim] // shards_of).reshape([-1 if axis == dim else 1 for axis in range(len(extent))])
    return loudness


def assign_block(own_key, own, number, rows, number_of, top, limit, skew):
    ranking = jax.random.permutation(own_key, number_of)
    heavy_load, usual = load_shares(number_of, rows * top, limit, skew, True), load_shares(number_of, rows * top, limit, skew, False)
    places = jnp.arange(number_of)

    def named(tallies, offset_by):
        used = int((tallies > 0).sum())
        fixed = max(1, used // 4)
        moved = fixed + (places - fixed + offset_by * (used - fixed)) % max(1, number_of - fixed)
        return jnp.zeros((number_of,), jnp.int32).at[ranking[jnp.where(places < fixed, places, moved)]].set(jnp.asarray(tallies, jnp.int32))

    tallies = jnp.where(number % 4 == 0, named(heavy_load, number // 4), named(usual, number - number // 4 - 1))
    mixed = jax.random.permutation(jax.random.fold_in(own, 3), number_of)
    donor, taker = mixed[0:number_of // 2 * 2:2], mixed[1:number_of // 2 * 2:2]
    slack = jnp.minimum(tallies[donor] - 1, limit - tallies[taker]) // 2
    slack = jnp.where((donor == ranking[0]) | (taker == ranking[0]) | (tallies[taker] == 0), 0, jnp.maximum(slack, 0))
    moved = jax.random.randint(jax.random.fold_in(own, 4), (number_of // 2,), 0, 1 << 20) % (slack + 1)
    tallies = tallies.at[donor].add(-moved).at[taker].add(moved)
    labels = jnp.searchsorted(jnp.cumsum(tallies), jnp.arange(rows * top), side="right").astype(jnp.int32)
    listing = labels.reshape(top, rows).T
    listing = listing[jax.random.permutation(jax.random.fold_in(own, 1), rows)]
    offset_by = jax.random.randint(jax.random.fold_in(own, 2), (rows, 1), 0, top)
    return jnp.take_along_axis(listing, (jnp.arange(top)[None, :] + offset_by) % top, axis=1)


def load_shares(count, total, bound, skew, full):
    loads = [(1 << 20) // math.isqrt(grade ** skew) + 1 for grade in range(1, count + 1)]
    largest = bound if full else min(bound, max(-(-total // count), total * loads[0] // sum(loads)))
    least = 1 if total - largest >= count - 1 else 0
    holding, surplus = [largest] + [least] * (count - 1), total - largest - least * (count - 1)
    while surplus > 0:
        movable = [i for i in range(1, count) if holding[i] < largest] or [i for i in range(1, count) if holding[i] < bound]
        whole, left = sum([loads[i] for i in movable]), surplus
        for i in movable:
            addition = min(bound - holding[i], max(1, left * loads[i] // whole), surplus)
            holding[i] = holding[i] + addition
            surplus = surplus - addition
    return np.array(holding)


def gaussian(rng, dims, scale, most, cuts=(), held_as=jnp.bfloat16):
    loudness = levels(rng, dims, cuts, -0.22, 0.18) if cuts else 1.0
    values = jax.random.normal(rng, dims, jnp.float32) * scale * loudness
    return jnp.minimum(jnp.maximum(values, -most), most).astype(held_as)


def setup_inputs(seed: int = 0) -> dict:
    key_list = jax.random.split(jax.random.key(seed), 13)
    conv_input = gaussian(key_list[0], (CONTEXT_LENGTH, CHANNELS), 1.0, 6.0, ((0, 8), (1, 4)))
    conv_weight = gaussian(key_list[1], (CONV, CHANNELS), CONV ** -0.5, 3.0, ((1, 4),), jnp.float32)
    b_proj = gaussian(key_list[2], (CONTEXT_LENGTH, STATE), STATE ** -0.5, 0.5, ((0, 8),))
    c_proj = gaussian(key_list[3], (CONTEXT_LENGTH, STATE), 0.05, 0.29882812, ((0, 8),))
    log_decay = draw_log_decay(jax.random.fold_in(key_list[12], 71), 0)
    skip_gain = jnp.clip(0.5 + 1.0 * jax.random.uniform(key_list[5], (HEADS,), jnp.float32) ** levels(key_list[5], (HEADS,), ((0, 4),), -0.2, 0.2), 0.5, 1.5)
    grad_in = gaussian(key_list[6], (CONTEXT_LENGTH, CHANNELS), 1.0, 6.0, ((0, 8), (1, 4)))
    norm_gain = jnp.clip(1.0 + 0.18 * jax.random.normal(key_list[7], (CHANNELS,), jnp.float32), 0.1, 1.9)
    expert_ids_keys = jax.random.split(jax.random.fold_in(key_list[8], 1), CONTEXT_LENGTH // (TOK_DEV // N_EXP))
    expert_ids_turns = jax.random.permutation(jax.random.fold_in(key_list[8], 3), CONTEXT_LENGTH // (TOK_DEV // N_EXP))
    expert_ids = jax.vmap(lambda own, number: assign_block(jax.random.fold_in(key_list[8], 2), own, number, TOK_DEV // N_EXP, EXPERTS, TOPK, MOST, 2))(expert_ids_keys, expert_ids_turns).reshape((CONTEXT_LENGTH, TOPK))
    expert_weights = jnp.clip(0.1 + 0.9 * jax.random.uniform(key_list[9], (CONTEXT_LENGTH, TOPK), jnp.float32) ** levels(key_list[9], (CONTEXT_LENGTH, TOPK), ((0, 8),), -0.2, 0.2), 0.1, 1.0)
    up_weight = gaussian(key_list[10], (EXPERTS, CHANNELS, FF), CHANNELS ** -0.5, 0.09375, ((0, 4), (2, 8)))
    down_weight = gaussian(key_list[11], (EXPERTS, FF, CHANNELS), FF ** -0.5, 0.0546875, ((0, 4), (1, 8)))
    return {"conv_input": conv_input, "conv_weight": conv_weight, "b_proj": b_proj, "c_proj": c_proj, "log_decay": log_decay, "skip_gain": skip_gain, "grad_in": grad_in, "norm_gain": norm_gain, "expert_ids": expert_ids, "expert_weights": expert_weights, "up_weight": up_weight, "down_weight": down_weight}


HIGHEST = lax.Precision.HIGHEST
EPSILON = 1e-06

def conv_mix(extended, conv_weight):
    rows_out = extended.shape[0] - conv_weight.shape[0] + 1
    total = jnp.zeros((rows_out, extended.shape[1]), jnp.float32)
    for offset in range(conv_weight.shape[0]):
        total = total + conv_weight[offset][None, :] * extended[offset:offset + rows_out]
    return jax.nn.silu(total).astype(jnp.bfloat16)

def block_terms(decay_block, b_raw, c_raw):
    totals = jnp.cumsum(decay_block, axis=1)
    rows_here = totals.shape[1]
    causal = jnp.arange(rows_here)[:, None] >= jnp.arange(rows_here)[None, :]
    spread = jnp.where(causal[None], totals[:, :, None] - totals[:, None, :], 0.0)
    kernel = jnp.where(causal[None], jnp.exp(spread), 0.0) * jnp.dot(c_raw, b_raw.T, preferred_element_type=jnp.float32)[None]
    to_end = jnp.exp(totals[:, -1:] - totals)
    return (totals, kernel, to_end)

def normalize(rows_in, norm_gain):
    values = rows_in.astype(jnp.float32)
    scale = lax.rsqrt(lax.optimization_barrier(jnp.mean(values * values, axis=1, keepdims=True)) + EPSILON)
    return (values * scale * norm_gain[None, :]).astype(jnp.bfloat16)

def reference(conv_input, conv_weight, b_proj, c_proj, log_decay, skip_gain, grad_in, norm_gain, expert_ids, expert_weights, up_weight, down_weight):
    padded = jnp.concatenate([jnp.zeros((CONV - 1, CHANNELS), jnp.float32), conv_input.astype(jnp.float32)], axis=0)
    mixed_in = conv_mix(padded, conv_weight)
    inputs_all = mixed_in.astype(jnp.float32).reshape(N_CTX, TOK_DEV, HEADS, HEAD_DIM)
    b_raw_all = b_proj.reshape(N_CTX, TOK_DEV, STATE)
    c_raw_all = c_proj.reshape(N_CTX, TOK_DEV, STATE)
    b_all = b_raw_all.astype(jnp.float32)
    c_all = c_raw_all.astype(jnp.float32)
    decays = log_decay.reshape(HEADS, N_CTX, TOK_DEV).transpose(1, 0, 2)
    grads_all = grad_in.astype(jnp.float32).reshape(N_CTX, TOK_DEV, HEADS, HEAD_DIM)

    def forward(carry_state, pieces):
        inputs_block, b_block, c_block, b_raw, c_raw, decay_block = pieces
        totals, kernel, to_end = block_terms(decay_block, b_raw, c_raw)
        inner = jnp.einsum('hts,shp->thp', kernel, inputs_block, precision=HIGHEST)
        carried = jnp.exp(totals).T[:, :, None] * jnp.einsum('hpn,tn->thp', carry_state, c_block, precision=HIGHEST)
        output = inner + carried + skip_gain[None, :, None] * inputs_block
        local_state = jnp.einsum('hs,shp,sn->hpn', to_end, inputs_block, b_block, precision=HIGHEST)
        carry_state = jnp.exp(totals[:, -1])[:, None, None] * carry_state + local_state
        return (carry_state, output)

    def backward(carry_grad, pieces):
        grad_block, b_block, c_block, b_raw, c_raw, decay_block = pieces
        totals, kernel, to_end = block_terms(decay_block, b_raw, c_raw)
        inner = jnp.einsum('hts,thp->shp', kernel, grad_block, precision=HIGHEST)
        carried = to_end.T[:, :, None] * jnp.einsum('hpn,sn->shp', carry_grad, b_block, precision=HIGHEST)
        result = inner + carried + skip_gain[None, :, None] * grad_block
        local_grad = jnp.einsum('ht,thp,tn->hpn', jnp.exp(totals), grad_block, c_block, precision=HIGHEST)
        carry_grad = jnp.exp(totals[:, -1])[:, None, None] * carry_grad + local_grad
        return (carry_grad, result)
    zero_state = jnp.zeros((HEADS, HEAD_DIM, STATE), jnp.float32)
    _, outputs = lax.scan(forward, zero_state, (inputs_all, b_all, c_all, b_raw_all, c_raw_all, decays))
    ssd_out = outputs.reshape(CONTEXT_LENGTH, CHANNELS).astype(jnp.bfloat16)
    _, grads_out = lax.scan(backward, zero_state, (grads_all, b_all, c_all, b_raw_all, c_raw_all, decays), reverse=True)
    grad_conv = grads_out.reshape(CONTEXT_LENGTH, CHANNELS)
    normed = normalize(ssd_out, norm_gain)
    flat_ids = expert_ids.reshape(-1)
    capacity = N_CTX * N_EXP * MOST
    order = jnp.arange(flat_ids.shape[0], dtype=jnp.int32)
    slice_width = FF // N_CTX

    def run_expert(expert):
        chosen = flat_ids == expert
        position = jnp.cumsum(chosen.astype(jnp.int32)) - 1
        target = jnp.where(chosen, position, capacity).astype(jnp.int32)
        source = jnp.zeros((capacity,), jnp.int32).at[target].set(order // TOPK, mode='drop')
        rows_in = normed[source].astype(jnp.float32)
        up_part = jnp.dot(rows_in, up_weight[expert].astype(jnp.float32), precision=HIGHEST)
        hidden = jax.nn.silu(up_part).astype(jnp.bfloat16)
        hidden_slices = hidden.reshape(capacity, N_CTX, slice_width).transpose(1, 0, 2)
        down_slices = down_weight[expert].reshape(N_CTX, slice_width, CHANNELS)

        def add_slice(total, pair):
            partial_sum = jnp.dot(pair[0].astype(jnp.float32), pair[1].astype(jnp.float32), precision=HIGHEST).astype(jnp.bfloat16)
            return (total + lax.optimization_barrier(partial_sum).astype(jnp.float32), None)
        total, _ = lax.scan(add_slice, jnp.zeros((capacity, CHANNELS), jnp.float32), (hidden_slices, down_slices))
        return total.astype(jnp.bfloat16)
    expert_outs = lax.map(run_expert, jnp.arange(EXPERTS, dtype=jnp.int32))
    onehot = (flat_ids[:, None] == jnp.arange(EXPERTS, dtype=jnp.int32)[None, :]).astype(jnp.int32)
    ranks = lax.optimization_barrier(jnp.sum((jnp.cumsum(onehot, axis=0) - 1) * onehot, axis=1)).astype(jnp.int32)
    pair_values = expert_outs[flat_ids, ranks].astype(jnp.float32).reshape(CONTEXT_LENGTH, TOPK, CHANNELS)
    moe_out = lax.optimization_barrier(jnp.sum(expert_weights[:, :, None] * pair_values, axis=1)).astype(jnp.bfloat16)
    return (moe_out, grad_conv)
```

```python
import jax
import jax.numpy as jnp
from jax import lax
from jax.experimental import pallas as pl
from jax.experimental.pallas import tpu as pltpu
from jax.sharding import PartitionSpec as P

CONV = 4
TOPK = 2


HIGHEST = lax.Precision.HIGHEST
EPSILON = 1e-06


def passed_along(block, axis, distance):
    devices = range(lax.axis_size(axis))
    route = [(i - distance, i) for i in devices if i - distance in devices]
    return lax.ppermute(block, axis, route)


def prefix(x, axis, combine, identity, reverse):
    size, mine = (lax.axis_size(axis), lax.axis_index(axis))
    everything = jax.tree.map(
        lambda part, kind: lax.all_gather(part.astype(kind), axis), x, (jnp.bfloat16, jnp.bfloat16)
    )
    start = jax.tree.map(
        lambda part, zero: jnp.broadcast_to(jnp.asarray(zero, part.dtype), part.shape), x, identity
    )

    def turn(k, before):
        at = size - 1 - k if reverse else k
        reached = at > mine if reverse else at < mine
        new = combine(
            before, jax.tree.map(lambda part, own: part[at].astype(own.dtype), everything, x)
        )
        return jax.tree.map(lambda a, b: jnp.where(reached, a, b), new, before)

    return lax.fori_loop(0, size, turn, start)


def combine_state(earlier, later):
    return (earlier[0] * later[0], later[0][:, None, None] * earlier[1] + later[1])


def conv_mix(extended, conv_weight):
    rows_out = extended.shape[0] - conv_weight.shape[0] + 1
    total = jnp.zeros((rows_out, extended.shape[1]), jnp.float32)
    for offset in range(conv_weight.shape[0]):
        total = total + conv_weight[offset][None, :] * extended[offset : offset + rows_out]
    return jax.nn.silu(total).astype(jnp.bfloat16)


def block_terms(decay_block, b_raw, c_raw):
    totals = jnp.cumsum(decay_block, axis=1)
    rows_here = totals.shape[1]
    causal = jnp.arange(rows_here)[:, None] >= jnp.arange(rows_here)[None, :]
    spread = jnp.where(causal[None], totals[:, :, None] - totals[:, None, :], 0.0)
    kernel = (
        jnp.where(causal[None], jnp.exp(spread), 0.0)
        * jnp.dot(c_raw, b_raw.T, preferred_element_type=jnp.float32)[None]
    )
    to_end = jnp.exp(totals[:, -1:] - totals)
    return (totals, kernel, to_end)


def normalize(rows_in, norm_gain):
    values = rows_in.astype(jnp.float32)
    scale = lax.rsqrt(jnp.mean(values * values, axis=1, keepdims=True) + EPSILON)
    return (values * scale * norm_gain[None, :]).astype(jnp.bfloat16)


def route_matrix(chosen_ids, slots_each, experts):
    pairs = chosen_ids.reshape(-1)
    onehot = (pairs[:, None] == jnp.arange(experts, dtype=jnp.int32)[None, :]).astype(jnp.int32)
    ranks = jnp.sum((jnp.cumsum(onehot, axis=0) - 1) * onehot, axis=1)
    target = pairs * slots_each + ranks
    return (jnp.arange(experts * slots_each, dtype=jnp.int32)[:, None] == target[None, :]).astype(
        jnp.bfloat16
    )


def gather_back(dispatch, returned, weights):
    values = jnp.einsum("sp,sc->pc", dispatch, returned, preferred_element_type=jnp.float32)
    values = values.reshape(weights.shape[0], weights.shape[1], returned.shape[1])
    return jnp.sum(weights[:, :, None] * values, axis=1).astype(jnp.bfloat16)


def expert_block(rows_in, up_weight, down_weight):
    up_local = up_weight[0]
    down_local = down_weight[0]
    hidden = jax.nn.silu(
        jnp.dot(
            lax.all_gather(rows_in, "ctx", axis=0, tiled=True),
            up_local,
            preferred_element_type=jnp.float32,
        )
    ).astype(jnp.bfloat16)
    summed = lax.psum_scatter(
        jnp.dot(hidden, down_local, preferred_element_type=jnp.float32).astype(jnp.bfloat16),
        "ctx",
        scatter_dimension=0,
        tiled=True,
    )
    return summed


def general_shards(
    conv_input,
    conv_weight,
    b_proj,
    c_proj,
    log_decay,
    skip_gain,
    grad_in,
    norm_gain,
    expert_ids,
    expert_weights,
    up_weight,
    down_weight,
):
    tok_rows = conv_input.shape[0]
    heads_here = log_decay.shape[0]
    head_size = conv_input.shape[1] // heads_here
    rim_rows = passed_along(conv_input[tok_rows - (CONV - 1) :], "ctx", 1)
    extended = jnp.concatenate(
        [rim_rows.astype(jnp.float32), conv_input.astype(jnp.float32)], axis=0
    )
    mixed_in = conv_mix(extended, conv_weight)
    inputs_block = mixed_in.astype(jnp.float32).reshape(tok_rows, heads_here, head_size)
    b_block = b_proj.astype(jnp.float32)
    c_block = c_proj.astype(jnp.float32)
    grad_block = grad_in.astype(jnp.float32).reshape(tok_rows, heads_here, head_size)
    totals, kernel, to_end = block_terms(log_decay, b_proj, c_proj)
    through = jnp.exp(totals[:, -1])
    local_state = jnp.einsum("hs,shp,sn->hpn", to_end, inputs_block, b_block, precision=HIGHEST)
    local_grad = jnp.einsum(
        "ht,thp,tn->hpn", jnp.exp(totals), grad_block, c_block, precision=HIGHEST
    )
    zero_state = jnp.zeros_like(local_state)
    ones_heads = jnp.ones_like(through)
    carry_state = prefix(
        (through, local_state), "ctx", combine_state, (ones_heads, zero_state), False
    )[1]
    carry_grad = prefix(
        (through, local_grad), "ctx", combine_state, (ones_heads, zero_state), True
    )[1]
    inner = jnp.einsum("hts,shp->thp", kernel, inputs_block, precision=HIGHEST)
    carried = jnp.exp(totals).T[:, :, None] * jnp.einsum(
        "hpn,tn->thp", carry_state, c_block, precision=HIGHEST
    )
    output = inner + carried + skip_gain[None, :, None] * inputs_block
    ssd_out = output.reshape(tok_rows, heads_here * head_size).astype(jnp.bfloat16)
    grad_inner = jnp.einsum("hts,thp->shp", kernel, grad_block, precision=HIGHEST)
    grad_carried = to_end.T[:, :, None] * jnp.einsum(
        "hpn,sn->shp", carry_grad, b_block, precision=HIGHEST
    )
    grad_conv = (grad_inner + grad_carried + skip_gain[None, :, None] * grad_block).reshape(
        tok_rows, heads_here * head_size
    )
    experts = lax.axis_size("exp")
    most_rows = 3 * TOPK * tok_rows // (2 * experts * experts)
    share = tok_rows // experts
    token_view = lax.all_to_all(ssd_out, "exp", split_axis=0, concat_axis=1, tiled=True)
    normed = normalize(token_view, norm_gain)
    first_row = lax.axis_index("exp") * share
    my_ids = lax.dynamic_slice_in_dim(expert_ids, first_row, share, 0)
    my_weights = lax.dynamic_slice_in_dim(expert_weights, first_row, share, 0)
    dispatch = route_matrix(my_ids, most_rows, experts)
    outgoing = jnp.dot(
        dispatch, jnp.repeat(normed, TOPK, axis=0), preferred_element_type=jnp.float32
    ).astype(jnp.bfloat16)
    incoming = lax.all_to_all(
        outgoing.reshape(experts, most_rows, normed.shape[1]),
        "exp",
        split_axis=0,
        concat_axis=0,
        tiled=True,
    )
    results = expert_block(
        incoming.reshape(experts * most_rows, normed.shape[1]), up_weight, down_weight
    )
    returned = lax.all_to_all(
        results.reshape(experts, most_rows, normed.shape[1]),
        "exp",
        split_axis=0,
        concat_axis=0,
        tiled=True,
    )
    combined = gather_back(
        dispatch, returned.reshape(experts * most_rows, normed.shape[1]), my_weights
    )
    moe_out = lax.all_to_all(combined, "exp", split_axis=1, concat_axis=0, tiled=True)
    return (moe_out, grad_conv)


CHUNKS = 2
DECAY_ROWS = 16
RIM = 8
F32 = jnp.float32
BF16 = jnp.bfloat16


def shape_of(shape, dtype):
    return jax.ShapeDtypeStruct(shape, dtype)


def call(body, outs, smem=0, scratch=(), cost=None, limit=40):
    def run(*args):
        specs = [pl.BlockSpec(memory_space=pltpu.SMEM)] * smem
        specs += [pl.BlockSpec(memory_space=pltpu.VMEM)] * (len(args) - smem)
        return pl.pallas_call(
            body,
            out_shape=outs,
            in_specs=specs,
            out_specs=jax.tree.map(lambda _: pl.BlockSpec(memory_space=pltpu.VMEM), outs),
            scratch_shapes=scratch,
            cost_estimate=cost,
            compiler_params=pltpu.CompilerParams(vmem_limit_bytes=limit << 20),
        )(*args)

    return run


def swap(x, axis, mask):
    size = lax.axis_size(axis)
    return lax.ppermute(x, axis, [(i, i ^ mask) for i in range(size)])


def exact_dot(a, b, dims=(((1,), (0,)), ((), ()))):
    return lax.dot_general(a, b, dims, precision=HIGHEST, preferred_element_type=F32)


def fast_dot(a, b):
    return jnp.dot(a, b, preferred_element_type=F32)


def iota(shape, dim):
    return lax.broadcasted_iota(jnp.int32, shape, dim)


def decay_columns(decay):
    rows = decay.shape[1]
    tri = (iota((rows, rows), 0) >= iota((rows, rows), 1)).astype(F32)
    return exact_dot(tri, decay, (((1,), (1,)), ((), ())))


def mix_kernel(core, conv, rim, taps, b, c, decay, grad, mixed_out, sent, kept, grow, fade):
    heads = decay.shape[0]
    rows, lanes = conv.shape
    x = conv[...].astype(F32)
    extended = jnp.concatenate([rim[...].astype(F32), x], axis=0)
    total = jnp.zeros((rows, lanes), F32)
    for tap in range(CONV):
        start = RIM - (CONV - 1) + tap
        total = total + taps[tap : tap + 1, :] * extended[start : start + rows]
    mixed = (total * jax.nn.sigmoid(total)).astype(BF16)
    mixed_out[...] = mixed
    columns = decay_columns(decay[...])
    width = lanes // heads
    spread = (iota((heads, lanes), 1) // width == iota((heads, lanes), 0)).astype(F32)
    totals = exact_dot(columns, spread)
    last = totals[rows - 1 : rows, :]
    growing = jnp.exp(totals)
    fading = jnp.exp(last - totals)
    grow[...] = growing
    fade[...] = fading
    through = jnp.broadcast_to(jnp.exp(last), (DECAY_ROWS, lanes)).astype(BF16)
    states = b.shape[1]
    forward = fast_dot(b[...].T, (fading * mixed.astype(F32)).astype(BF16)).astype(BF16)
    backward = fast_dot(c[...].T, (growing * grad[...].astype(F32)).astype(BF16)).astype(BF16)
    first = core[0] == 0
    sent[0:states, :] = jnp.where(first, forward, backward)
    kept[0:states, :] = jnp.where(first, backward, forward)
    sent[states:, :] = through
    kept[states:, :] = through


def pair_kernel(received, kept, chip):
    states = kept.shape[0] - DECAY_ROWS
    decay = kept[states : states + 1, :].astype(F32)
    got = received[0:states, :].astype(F32)
    chip[0:states, :] = (got * decay + kept[0:states, :].astype(F32)).astype(BF16)
    both = decay * received[states : states + 1, :].astype(F32)
    chip[states:, :] = jnp.broadcast_to(both, (DECAY_ROWS, both.shape[1])).astype(BF16)


def reach_kernel(flip, near, middle, far, mine):
    states = mine.shape[0]
    flipped = flip[0] != 0

    def part(ref):
        return ref[0:states, :].astype(F32), ref[states : states + 1, :].astype(F32)

    a, a_decay = part(near)
    b, b_decay = part(middle)
    c, c_decay = part(far)
    first, first_decay = jnp.where(flipped, c, a), jnp.where(flipped, c_decay, a_decay)
    third = jnp.where(flipped, a, c)
    mine[...] = (first + first_decay * (b + b_decay * third)).astype(BF16)


def inner_kernel(mixed, b, c, decay, grad, skip, out, grad_out):
    heads, rows = decay.shape
    lanes = mixed.shape[1]
    width = lanes // heads
    pack = 128 // width
    columns = decay_columns(decay[...])
    tri_rows = (iota((rows, rows), 0) <= iota((rows, rows), 1)).astype(F32)
    totals = exact_dot(decay[...], tri_rows)
    nt = (((1,), (1,)), ((), ()))
    scores = lax.dot_general(c[...], b[...], nt, preferred_element_type=F32)
    flipped = lax.dot_general(b[...], c[...], nt, preferred_element_type=F32)
    t, s = iota((rows, rows), 0), iota((rows, rows), 1)
    spread = (iota((heads, lanes), 1) // width == iota((heads, lanes), 0)).astype(F32)
    gains = exact_dot(skip[...], spread)
    lane = iota((rows, 128), 1) // width
    for group in range(lanes // 128):
        at = slice(group * 128, group * 128 + 128)
        x = mixed[:, at]
        g = grad[:, at]
        left, right, xs, gs = [], [], [], []
        for k in range(pack):
            h = group * pack + k
            gap = columns[:, h : h + 1] - totals[h : h + 1, :]
            left.append((jnp.exp(jnp.where(t >= s, gap, -1e30)) * scores).astype(BF16))
            right.append((jnp.exp(jnp.where(t <= s, -gap, -1e30)) * flipped).astype(BF16))
            xs.append(jnp.where(lane == k, x, jnp.zeros_like(x)))
            gs.append(jnp.where(lane == k, g, jnp.zeros_like(g)))
        gain = gains[0:1, at]
        out[:, at] = fast_dot(jnp.concatenate(left, 1), jnp.concatenate(xs, 0)) + gain * x.astype(F32)
        grad_out[:, at] = fast_dot(jnp.concatenate(right, 1), jnp.concatenate(gs, 0)) + gain * g.astype(F32)


def choices(ids, mine, masks, rows, chunks):
    named = []
    for mask in range(masks):
        wanted = mine ^ mask
        named.append(((ids[0:1, :] == wanted) | (ids[1:2, :] == wanted)).astype(F32))
    named.append(jnp.zeros((8 - masks, rows), F32))
    names = jnp.concatenate(named, axis=0)
    before, after = iota((rows, rows), 0), iota((rows, rows), 1)
    share = rows // chunks
    tri = ((before <= after) & (before // share == after // share)).astype(BF16)
    return names, fast_dot(names.astype(BF16), tri).astype(jnp.int32)


def carry_kernel(core, mine, shared, prefix, received, inner, grow, c, ids, *outs):
    chunks, masks = len(outs) // N_MASKS, N_MASKS
    states, lanes = prefix.shape
    rows = inner.shape[0]
    own = carried(prefix, received)
    carry = jnp.where(core[0] != 0, own, shared[...].astype(F32))
    out = inner[...] + grow[...] * fast_dot(c[...], carry.astype(BF16))
    out = out.astype(BF16)
    names, counts = choices(ids[...], mine[0], masks, rows, chunks)
    slots = outs[0].shape[0]
    chunk_of = iota((slots, rows), 1) // (rows // chunks)
    slot = iota((slots, rows), 0)
    for chunk in range(chunks):
        for mask in range(masks):
            row = (counts[mask : mask + 1, :] - 1 == slot) & (names[mask : mask + 1, :] > 0)
            pick = (row & (chunk_of == chunk)).astype(BF16)
            outs[chunk * masks + mask][...] = fast_dot(pick, out).astype(BF16)


def carried(prefix, received):
    states = prefix.shape[0]
    decay = received[states : states + 1, :].astype(F32)
    return prefix[...].astype(F32) * decay + received[0:states, :].astype(F32)


def grad_kernel(core, shared, prefix, received, inner, fade, b, out):
    own = carried(prefix, received)
    carry = jnp.where(core[0] != 0, shared[...].astype(F32), own)
    out[...] = inner[...] + fade[...] * fast_dot(b[...], carry.astype(BF16))


N_MASKS = 4


def norm_kernel(mine, gain, *refs):
    parts, out = refs[:-1], refs[-1]
    width = parts[0].shape[1]
    features = width * len(parts)
    values = [part[...].astype(F32) for part in parts]
    squares = sum(jnp.sum(v * v, axis=1, keepdims=True) for v in values)
    scale = lax.rsqrt(squares / features + EPSILON)
    per_half = len(parts) // 2
    for mask, value in enumerate(values):
        at = mine[0] ^ mask
        to = pl.multiple_of((at % per_half) * width, width)
        gains = gain[:, pl.ds(pl.multiple_of(at * width, width), width)]
        out[at // per_half, :, pl.ds(to, width)] = (value * scale * gains).astype(BF16)


def ffn_kernel(n_up, split, *refs):
    blocks, (up, down, even, odd, rows_in, hidden, sems) = refs[:-7], refs[-7:]
    step = pl.program_id(0)
    slots = blocks[0].shape[-2]
    half = rows_in.shape[1] // 2

    @pl.when(step == 0)
    def _():
        copies = []
        for n, (place, part) in enumerate(split):
            at = rows_in.at[pl.ds(place * slots, slots)]
            if part is None:
                for side in range(2):
                    copies.append(
                        pltpu.make_async_copy(
                            blocks[n].at[side], at.at[:, pl.ds(side * half, half)], sems.at[len(copies)]
                        )
                    )
            else:
                copies.append(
                    pltpu.make_async_copy(
                        blocks[n], at.at[:, pl.ds(part * half, half)], sems.at[len(copies)]
                    )
                )
        for copy in copies:
            copy.start()
        for copy in copies:
            copy.wait()

    @pl.when(step < n_up)
    def _():
        value = fast_dot(rows_in[...], up[...])
        width = up.shape[1]
        to = pl.multiple_of(step * width, width)
        hidden[:, pl.ds(to, width)] = (value * jax.nn.sigmoid(value)).astype(BF16)

    @pl.when(step >= n_up)
    def _():
        value = fast_dot(hidden[...], down[...]).astype(BF16)
        count = even.shape[0] * slots
        even[...] = value[:count].reshape(even.shape)
        odd[...] = value[count:].reshape(odd.shape)


UP_TILE = 256
DOWN_TILE = 512


def expert_rows(blocks, split, places, up, down):
    slots, half = blocks[0].shape[-2:]
    features, hidden = up.shape
    n_up, n_down = hidden // UP_TILE, features // DOWN_TILE
    per_half = half // DOWN_TILE
    rows = places * slots

    def out_at(i):
        j = jnp.maximum(i - n_up, 0)
        return (0, j // per_half, 0, j % per_half)

    spec = pl.BlockSpec((places // 2, None, slots, DOWN_TILE), out_at)
    n_copies = sum(2 if part is None else 1 for _, part in split)
    return pl.pallas_call(
        lambda *refs: ffn_kernel(n_up, split, *refs),
        grid=(n_up + n_down,),
        in_specs=[pl.BlockSpec(memory_space=pl.ANY)] * len(blocks)
        + [
            pl.BlockSpec((features, UP_TILE), lambda i: (0, jnp.minimum(i, n_up - 1))),
            pl.BlockSpec((hidden, DOWN_TILE), lambda i: (0, jnp.maximum(i - n_up, 0))),
        ],
        out_specs=[spec, spec],
        out_shape=[shape_of((places // 2, 2, slots, half), BF16)] * 2,
        scratch_shapes=[
            pltpu.VMEM((rows, features), BF16),
            pltpu.VMEM((rows, hidden), BF16),
            pltpu.SemaphoreType.DMA((n_copies,)),
        ],
        cost_estimate=pl.CostEstimate(
            flops=4 * rows * features * hidden,
            transcendentals=rows * hidden,
            bytes_accessed=4 * features * hidden + 4 * rows * features,
        ),
        compiler_params=pltpu.CompilerParams(
            dimension_semantics=("arbitrary",), vmem_limit_bytes=48 << 20
        ),
    )(*blocks, up, down)


def both(a, b):
    return (a.astype(F32) + b.astype(F32)).astype(BF16)


def chip_sum_kernel(even, other, own, to_x, to_y, rest_x, rest_y):
    own[...] = both(even[0], other[0])
    to_x[0] = both(even[3, 0], other[3, 0])
    to_y[0] = both(even[3, 1], other[3, 1])
    to_x[1] = both(even[1, 0], other[1, 0])
    to_y[1] = both(even[2, 1], other[2, 1])
    rest_x[...] = both(even[1, 1], other[1, 1])
    rest_y[...] = both(even[2, 0], other[2, 0])


def relay_kernel(from_x, from_y, rest_x, rest_y, next_x, next_y):
    next_x[...] = both(rest_x[...], from_y[0])
    next_y[...] = both(rest_y[...], from_x[0])


def total_kernel(mine, own, from_x, from_y, last_x, last_y, *refs):
    outs, total = refs[:-1], refs[-1]
    width = outs[0].shape[1]
    per_half = len(outs) // 2

    def add(a, b, c):
        return (a.astype(F32) + b.astype(F32) + c.astype(F32)).astype(BF16)

    total[0] = add(own[0], from_x[1], last_y[...])
    total[1] = add(own[1], last_x[...], from_y[1])
    for mask, out in enumerate(outs):
        at = mine[0] ^ mask
        to = pl.multiple_of((at % per_half) * width, width)
        out[...] = total[at // per_half, :, pl.ds(to, width)]


def combine_kernel(mine, ids, weights, *refs):
    parts, out = refs[:-1], refs[-1]
    masks = N_MASKS
    chunks = len(parts) // masks
    slots = parts[0].shape[0]
    rows = out.shape[0]
    chosen = ids[...]
    names, counts = choices(chosen, mine[0], masks, rows, chunks)
    chunk_of = iota((slots, rows), 1) // (rows // chunks)
    slot = iota((slots, rows), 0)
    values = jnp.concatenate([part[...] for part in parts], axis=0)
    result = jnp.zeros(out.shape, F32)
    for k in range(TOPK):
        picks = []
        for chunk in range(chunks):
            for mask in range(masks):
                row = (counts[mask : mask + 1, :] - 1 == slot) & (chosen[k : k + 1, :] == mine[0] ^ mask)
                picks.append((row & (chunk_of == chunk)).astype(F32))
        pick = jnp.concatenate(picks, axis=0).T.astype(BF16)
        result = result + weights[:, k : k + 1] * fast_dot(pick, values)
    out[...] = result.astype(BF16)


def directed(x, mask):
    size = lax.axis_size("ctx")
    route = []
    for i in range(size):
        j = i ^ mask
        if (j > i) == (i % 2 == 1):
            route.append((i, j))
    return lax.ppermute(x, "ctx", route)


def exchange_shards(
    conv_input,
    conv_weight,
    b_proj,
    c_proj,
    log_decay,
    skip_gain,
    grad_in,
    norm_gain,
    expert_ids,
    expert_weights,
    up_weight,
    down_weight,
):
    rows, lanes = conv_input.shape
    heads = log_decay.shape[0]
    states = b_proj.shape[1]
    experts = lax.axis_size("exp")
    features = lanes * experts
    place = lax.axis_index("ctx")
    core = (place & 1).reshape(1)
    chip = place >> 1
    mine = lax.axis_index("exp").reshape(1)
    ids = expert_ids.T
    block = shape_of((rows, lanes), F32)
    payload = shape_of((states + DECAY_ROWS, lanes), BF16)

    rim = passed_along(conv_input[rows - RIM :], "ctx", 1)
    mixed, sent, kept, grow, fade = call(
        mix_kernel, [shape_of((rows, lanes), BF16), payload, payload, block, block], smem=1
    )(core, conv_input, rim, conv_weight, b_proj, c_proj, log_decay, grad_in)
    received = swap(sent, "ctx", 1)
    chip_sum = call(pair_kernel, payload)(received, kept)
    near, middle, far = (directed(chip_sum, mask) for mask in (2, 4, 6))
    inner, grad_inner = call(inner_kernel, [block, block])(
        mixed, b_proj, c_proj, log_decay, grad_in, skip_gain.reshape(1, heads)
    )
    later = place & 1
    flip = jnp.where(later == 1, chip == 2, chip == 1).astype(jnp.int32).reshape(1)
    prefix = call(reach_kernel, shape_of((states, lanes), BF16), smem=1)(flip, near, middle, far)
    shared = swap(prefix, "ctx", 1)

    slots = 3 * TOPK * rows // (2 * experts * CHUNKS)
    picked = call(carry_kernel, [shape_of((slots, lanes), BF16)] * (CHUNKS * experts), smem=2)(
        core, mine, shared, prefix, received, inner, grow, c_proj, ids
    )
    grad_conv = call(grad_kernel, block, smem=1)(
        core, shared, prefix, received, grad_inner, fade, b_proj
    )

    gain = norm_gain.reshape(1, features)
    half = features // 2
    row_block = shape_of((2, slots, half), BF16)
    half_block = shape_of((slots, half), BF16)
    up_local, down_local = up_weight[0], down_weight[0]
    split = [(0, None), (4, None), (1, None), (5, None), (2, None), (6, None), (3, 0), (7, 0), (3, 1), (7, 1)]
    returned = []
    for chunk in range(CHUNKS):
        parts = picked[chunk * experts : (chunk + 1) * experts]
        arrived = [parts[0]] + [swap(parts[m], "exp", m) for m in range(1, experts)]
        own = call(norm_kernel, row_block, smem=1)(mine, gain, *arrived)
        twin = swap(own, "ctx", 1)
        along_x, along_y = swap(own, "ctx", 2), swap(own, "ctx", 4)
        diagonal = [swap(along_y[0], "ctx", 2), swap(along_x[1], "ctx", 4)]
        blocks = [own, twin]
        for block_in in (along_x, along_y, *diagonal):
            blocks += [block_in, swap(block_in, "ctx", 1)]
        even, odd = expert_rows(blocks, split, 8, up_local, down_local)
        other = swap(odd, "ctx", 1)
        own_sum, to_x, to_y, rest_x, rest_y = call(
            chip_sum_kernel, [row_block, row_block, row_block, half_block, half_block]
        )(even, other)
        from_x, from_y = swap(to_x, "ctx", 2), swap(to_y, "ctx", 4)
        next_x, next_y = call(relay_kernel, [half_block, half_block])(from_x, from_y, rest_x, rest_y)
        last_x, last_y = swap(next_x, "ctx", 2), swap(next_y, "ctx", 4)
        results = call(
            total_kernel,
            [shape_of((slots, lanes), BF16)] * experts,
            smem=1,
            scratch=[pltpu.VMEM((2, slots, half), BF16)],
        )(mine, own_sum, from_x, from_y, last_x, last_y)
        returned += [results[0]] + [swap(results[m], "exp", m) for m in range(1, experts)]
    moe_out = call(combine_kernel, shape_of((rows, lanes), BF16), smem=1)(
        mine, ids, expert_weights, *returned
    )
    return (moe_out, grad_conv)


def solution(mesh):
    placed = (
        P("ctx", "exp"),
        P(None, "exp"),
        P("ctx", None),
        P("ctx", None),
        P("exp", "ctx"),
        P("exp"),
        P("ctx", "exp"),
        P(),
        P("ctx", None),
        P("ctx", None),
        P("exp", None, "ctx"),
        P("exp", "ctx", None),
    )
    swaps = mesh.shape["ctx"] == 8 and mesh.shape["exp"] == 4
    return jax.shard_map(
        exchange_shards if swaps else general_shards,
        mesh=mesh,
        in_specs=placed,
        out_specs=(P("ctx", "exp"), P("ctx", "exp")),
        check_vma=False,
    )
```

```python
import jax
import jax.numpy as jnp
from jax import lax
from jax.experimental import pallas as pl
from jax.experimental.pallas import tpu as pltpu
from jax.sharding import PartitionSpec as P

CONV = 4
TOPK = 2


HIGHEST = lax.Precision.HIGHEST
EPSILON = 1e-06


def passed_along(block, axis, distance):
    devices = range(lax.axis_size(axis))
    route = [(i - distance, i) for i in devices if i - distance in devices]
    return lax.ppermute(block, axis, route)


def prefix(x, axis, combine, identity, reverse):
    size, mine = (lax.axis_size(axis), lax.axis_index(axis))
    everything = jax.tree.map(
        lambda part, kind: lax.all_gather(part.astype(kind), axis), x, (jnp.bfloat16, jnp.bfloat16)
    )
    start = jax.tree.map(
        lambda part, zero: jnp.broadcast_to(jnp.asarray(zero, part.dtype), part.shape), x, identity
    )

    def turn(k, before):
        at = size - 1 - k if reverse else k
        reached = at > mine if reverse else at < mine
        new = combine(
            before, jax.tree.map(lambda part, own: part[at].astype(own.dtype), everything, x)
        )
        return jax.tree.map(lambda a, b: jnp.where(reached, a, b), new, before)

    return lax.fori_loop(0, size, turn, start)


def combine_state(earlier, later):
    return (earlier[0] * later[0], later[0][:, None, None] * earlier[1] + later[1])


def conv_mix(extended, conv_weight):
    rows_out = extended.shape[0] - conv_weight.shape[0] + 1
    total = jnp.zeros((rows_out, extended.shape[1]), jnp.float32)
    for offset in range(conv_weight.shape[0]):
        total = total + conv_weight[offset][None, :] * extended[offset : offset + rows_out]
    return jax.nn.silu(total).astype(jnp.bfloat16)


def block_terms(decay_block, b_raw, c_raw):
    totals = jnp.cumsum(decay_block, axis=1)
    rows_here = totals.shape[1]
    causal = jnp.arange(rows_here)[:, None] >= jnp.arange(rows_here)[None, :]
    spread = jnp.where(causal[None], totals[:, :, None] - totals[:, None, :], 0.0)
    kernel = (
        jnp.where(causal[None], jnp.exp(spread), 0.0)
        * jnp.dot(c_raw, b_raw.T, preferred_element_type=jnp.float32)[None]
    )
    to_end = jnp.exp(totals[:, -1:] - totals)
    return (totals, kernel, to_end)


def normalize(rows_in, norm_gain):
    values = rows_in.astype(jnp.float32)
    scale = lax.rsqrt(jnp.mean(values * values, axis=1, keepdims=True) + EPSILON)
    return (values * scale * norm_gain[None, :]).astype(jnp.bfloat16)


def route_matrix(chosen_ids, slots_each, experts):
    pairs = chosen_ids.reshape(-1)
    onehot = (pairs[:, None] == jnp.arange(experts, dtype=jnp.int32)[None, :]).astype(jnp.int32)
    ranks = jnp.sum((jnp.cumsum(onehot, axis=0) - 1) * onehot, axis=1)
    target = pairs * slots_each + ranks
    return (jnp.arange(experts * slots_each, dtype=jnp.int32)[:, None] == target[None, :]).astype(
        jnp.bfloat16
    )


def gather_back(dispatch, returned, weights):
    values = jnp.einsum("sp,sc->pc", dispatch, returned, preferred_element_type=jnp.float32)
    values = values.reshape(weights.shape[0], weights.shape[1], returned.shape[1])
    return jnp.sum(weights[:, :, None] * values, axis=1).astype(jnp.bfloat16)


def expert_block(rows_in, up_weight, down_weight):
    up_local = up_weight[0]
    down_local = down_weight[0]
    hidden = jax.nn.silu(
        jnp.dot(
            lax.all_gather(rows_in, "ctx", axis=0, tiled=True),
            up_local,
            preferred_element_type=jnp.float32,
        )
    ).astype(jnp.bfloat16)
    summed = lax.psum_scatter(
        jnp.dot(hidden, down_local, preferred_element_type=jnp.float32).astype(jnp.bfloat16),
        "ctx",
        scatter_dimension=0,
        tiled=True,
    )
    return summed


def general_shards(
    conv_input,
    conv_weight,
    b_proj,
    c_proj,
    log_decay,
    skip_gain,
    grad_in,
    norm_gain,
    expert_ids,
    expert_weights,
    up_weight,
    down_weight,
):
    tok_rows = conv_input.shape[0]
    heads_here = log_decay.shape[0]
    head_size = conv_input.shape[1] // heads_here
    rim_rows = passed_along(conv_input[tok_rows - (CONV - 1) :], "ctx", 1)
    extended = jnp.concatenate(
        [rim_rows.astype(jnp.float32), conv_input.astype(jnp.float32)], axis=0
    )
    mixed_in = conv_mix(extended, conv_weight)
    inputs_block = mixed_in.astype(jnp.float32).reshape(tok_rows, heads_here, head_size)
    b_block = b_proj.astype(jnp.float32)
    c_block = c_proj.astype(jnp.float32)
    grad_block = grad_in.astype(jnp.float32).reshape(tok_rows, heads_here, head_size)
    totals, kernel, to_end = block_terms(log_decay, b_proj, c_proj)
    through = jnp.exp(totals[:, -1])
    local_state = jnp.einsum("hs,shp,sn->hpn", to_end, inputs_block, b_block, precision=HIGHEST)
    local_grad = jnp.einsum(
        "ht,thp,tn->hpn", jnp.exp(totals), grad_block, c_block, precision=HIGHEST
    )
    zero_state = jnp.zeros_like(local_state)
    ones_heads = jnp.ones_like(through)
    carry_state = prefix(
        (through, local_state), "ctx", combine_state, (ones_heads, zero_state), False
    )[1]
    carry_grad = prefix(
        (through, local_grad), "ctx", combine_state, (ones_heads, zero_state), True
    )[1]
    inner = jnp.einsum("hts,shp->thp", kernel, inputs_block, precision=HIGHEST)
    carried = jnp.exp(totals).T[:, :, None] * jnp.einsum(
        "hpn,tn->thp", carry_state, c_block, precision=HIGHEST
    )
    output = inner + carried + skip_gain[None, :, None] * inputs_block
    ssd_out = output.reshape(tok_rows, heads_here * head_size).astype(jnp.bfloat16)
    grad_inner = jnp.einsum("hts,thp->shp", kernel, grad_block, precision=HIGHEST)
    grad_carried = to_end.T[:, :, None] * jnp.einsum(
        "hpn,sn->shp", carry_grad, b_block, precision=HIGHEST
    )
    grad_conv = (grad_inner + grad_carried + skip_gain[None, :, None] * grad_block).reshape(
        tok_rows, heads_here * head_size
    )
    experts = lax.axis_size("exp")
    most_rows = 3 * TOPK * tok_rows // (2 * experts * experts)
    share = tok_rows // experts
    token_view = lax.all_to_all(ssd_out, "exp", split_axis=0, concat_axis=1, tiled=True)
    normed = normalize(token_view, norm_gain)
    first_row = lax.axis_index("exp") * share
    my_ids = lax.dynamic_slice_in_dim(expert_ids, first_row, share, 0)
    my_weights = lax.dynamic_slice_in_dim(expert_weights, first_row, share, 0)
    dispatch = route_matrix(my_ids, most_rows, experts)
    outgoing = jnp.dot(
        dispatch, jnp.repeat(normed, TOPK, axis=0), preferred_element_type=jnp.float32
    ).astype(jnp.bfloat16)
    incoming = lax.all_to_all(
        outgoing.reshape(experts, most_rows, normed.shape[1]),
        "exp",
        split_axis=0,
        concat_axis=0,
        tiled=True,
    )
    results = expert_block(
        incoming.reshape(experts * most_rows, normed.shape[1]), up_weight, down_weight
    )
    returned = lax.all_to_all(
        results.reshape(experts, most_rows, normed.shape[1]),
        "exp",
        split_axis=0,
        concat_axis=0,
        tiled=True,
    )
    combined = gather_back(
        dispatch, returned.reshape(experts * most_rows, normed.shape[1]), my_weights
    )
    moe_out = lax.all_to_all(combined, "exp", split_axis=1, concat_axis=0, tiled=True)
    return (moe_out, grad_conv)


CHUNKS = 2
LIGHT = pl.CostEstimate(flops=1, transcendentals=0, bytes_accessed=1)
DECAY_ROWS = 8
RIM = 8
F32 = jnp.float32
BF16 = jnp.bfloat16


def shape_of(shape, dtype):
    return jax.ShapeDtypeStruct(shape, dtype)


def call(body, outs, smem=0, scratch=(), limit=6):
    def run(*args):
        specs = [pl.BlockSpec(memory_space=pltpu.SMEM)] * smem
        specs += [pl.BlockSpec(memory_space=pltpu.VMEM)] * (len(args) - smem)
        return pl.pallas_call(
            body,
            out_shape=outs,
            in_specs=specs,
            out_specs=jax.tree.map(lambda _: pl.BlockSpec(memory_space=pltpu.VMEM), outs),
            scratch_shapes=scratch,
            cost_estimate=LIGHT,
            compiler_params=pltpu.CompilerParams(vmem_limit_bytes=limit << 20),
        )(*args)

    return run


def swap(x, axis, mask):
    size = lax.axis_size(axis)
    return lax.ppermute(x, axis, [(i, i ^ mask) for i in range(size)])


def exact_dot(a, b, dims=(((1,), (0,)), ((), ()))):
    return lax.dot_general(a, b, dims, precision=HIGHEST, preferred_element_type=F32)


def fast_dot(a, b):
    return jnp.dot(a, b, preferred_element_type=F32)


def iota(shape, dim):
    return lax.broadcasted_iota(jnp.int32, shape, dim)


def decay_columns(decay):
    rows = decay.shape[1]
    tri = (iota((rows, rows), 0) >= iota((rows, rows), 1)).astype(F32)
    return exact_dot(tri, decay, (((1,), (1,)), ((), ())))


def prepare_kernel(n, *refs):
    sources, held = refs[:n], refs[n : 2 * n]
    grow, fade, backward, through, sems = refs[2 * n :]
    copies = [pltpu.make_async_copy(a, b, sems.at[k]) for k, (a, b) in enumerate(zip(sources, held))]
    for copy in copies:
        copy.start()
    for copy in copies:
        copy.wait()
    decay, c, grad = held[:3]
    heads = decay.shape[0]
    rows, lanes = grad.shape
    columns = decay_columns(decay[...])
    width = lanes // heads
    spread = (iota((heads, lanes), 1) // width == iota((heads, lanes), 0)).astype(F32)
    totals = exact_dot(columns, spread)
    last = totals[rows - 1 : rows, :]
    growing = jnp.exp(totals)
    grow[...] = growing
    fade[...] = jnp.exp(last - totals)
    through[...] = jnp.broadcast_to(jnp.exp(last), (DECAY_ROWS, lanes)).astype(BF16)
    backward[...] = fast_dot(c[...].T, (growing * grad[...].astype(F32)).astype(BF16)).astype(BF16)


def mix_kernel(core, conv, rim, taps, b, fade, backward, through, mixed_out, sent, kept):
    rows, lanes = conv.shape
    x = conv[...].astype(F32)
    extended = jnp.concatenate([rim[...].astype(F32), x], axis=0)
    total = jnp.zeros((rows, lanes), F32)
    for tap in range(CONV):
        start = RIM - (CONV - 1) + tap
        total = total + taps[tap : tap + 1, :] * extended[start : start + rows]
    mixed = (total * jax.nn.sigmoid(total)).astype(BF16)
    mixed_out[...] = mixed
    states = b.shape[1]
    forward = fast_dot(b[...].T, (fade[...] * mixed.astype(F32)).astype(BF16)).astype(BF16)
    first = core[0] == 0
    sent[0:states, :] = jnp.where(first, forward, backward[...])
    kept[0:states, :] = jnp.where(first, backward[...], forward)
    sent[states:, :] = through[...]
    kept[states:, :] = through[...]


def load_kernel(source, held, sem):
    copy = pltpu.make_async_copy(source, held, sem)
    copy.start()
    copy.wait()


def load(source, limit):
    return pl.pallas_call(
        load_kernel,
        out_shape=pltpu.VMEM(source.shape, source.dtype),
        in_specs=[pl.BlockSpec(memory_space=pltpu.HBM)],
        out_specs=pl.BlockSpec(memory_space=pltpu.VMEM),
        scratch_shapes=[pltpu.SemaphoreType.DMA],
        cost_estimate=LIGHT,
        compiler_params=pltpu.CompilerParams(vmem_limit_bytes=limit << 20),
    )(pltpu.with_memory_space_constraint(source, pltpu.HBM))


def after(x, *others):
    return lax.optimization_barrier((x, *others))[0]


def pair_kernel(received, kept, chip):
    states = kept.shape[0] - DECAY_ROWS
    decay = kept[states : states + 1, :].astype(F32)
    got = received[0:states, :].astype(F32)
    chip[0:states, :] = (got * decay + kept[0:states, :].astype(F32)).astype(BF16)
    both = decay * received[states : states + 1, :].astype(F32)
    chip[states:, :] = jnp.broadcast_to(both, (DECAY_ROWS, both.shape[1])).astype(BF16)


def reach_kernel(flip, near, middle, far, mine):
    states = mine.shape[0]
    flipped = flip[0] != 0

    def part(ref):
        return ref[0:states, :].astype(F32), ref[states : states + 1, :].astype(F32)

    a, a_decay = part(near)
    b, b_decay = part(middle)
    c, c_decay = part(far)
    first, first_decay = jnp.where(flipped, c, a), jnp.where(flipped, c_decay, a_decay)
    third = jnp.where(flipped, a, c)
    mine[...] = (first + first_decay * (b + b_decay * third)).astype(BF16)


def inner_kernel(mixed, b, c, decay, grad, skip, out, grad_out):
    heads, rows = decay.shape
    lanes = mixed.shape[1]
    width = lanes // heads
    pack = 128 // width
    columns = decay_columns(decay[...])
    tri_rows = (iota((rows, rows), 0) <= iota((rows, rows), 1)).astype(F32)
    totals = exact_dot(decay[...], tri_rows)
    nt = (((1,), (1,)), ((), ()))
    scores = lax.dot_general(c[...], b[...], nt, preferred_element_type=F32)
    flipped = lax.dot_general(b[...], c[...], nt, preferred_element_type=F32)
    t, s = iota((rows, rows), 0), iota((rows, rows), 1)
    spread = (iota((heads, lanes), 1) // width == iota((heads, lanes), 0)).astype(F32)
    gains = exact_dot(skip[...], spread)
    lane = iota((rows, 128), 1) // width
    for group in range(lanes // 128):
        at = slice(group * 128, group * 128 + 128)
        x = mixed[:, at]
        g = grad[:, at]
        left, right, xs, gs = [], [], [], []
        for k in range(pack):
            h = group * pack + k
            gap = columns[:, h : h + 1] - totals[h : h + 1, :]
            left.append((jnp.exp(jnp.where(t >= s, gap, -1e30)) * scores).astype(BF16))
            right.append((jnp.exp(jnp.where(t <= s, -gap, -1e30)) * flipped).astype(BF16))
            xs.append(jnp.where(lane == k, x, jnp.zeros_like(x)))
            gs.append(jnp.where(lane == k, g, jnp.zeros_like(g)))
        gain = gains[0:1, at]
        out[:, at] = fast_dot(jnp.concatenate(left, 1), jnp.concatenate(xs, 0)) + gain * x.astype(F32)
        grad_out[:, at] = fast_dot(jnp.concatenate(right, 1), jnp.concatenate(gs, 0)) + gain * g.astype(F32)


def choices(ids, mine, masks, rows, chunks):
    named = []
    for mask in range(masks):
        wanted = mine ^ mask
        named.append(((ids[0:1, :] == wanted) | (ids[1:2, :] == wanted)).astype(F32))
    named.append(jnp.zeros((8 - masks, rows), F32))
    names = jnp.concatenate(named, axis=0)
    before, after = iota((rows, rows), 0), iota((rows, rows), 1)
    share = rows // chunks
    tri = ((before <= after) & (before // share == after // share)).astype(BF16)
    return names, fast_dot(names.astype(BF16), tri).astype(jnp.int32)


def carry_kernel(core, mine, shared, prefix, received, inner, grow, c, ids, *outs):
    chunks, masks = len(outs) // N_MASKS, N_MASKS
    states, lanes = prefix.shape
    rows = inner.shape[0]
    own = carried(prefix, received)
    carry = jnp.where(core[0] != 0, own, shared[...].astype(F32))
    out = inner[...] + grow[...] * fast_dot(c[...], carry.astype(BF16))
    out = out.astype(BF16)
    names, counts = choices(ids[...], mine[0], masks, rows, chunks)
    slots = outs[0].shape[0]
    chunk_of = iota((slots, rows), 1) // (rows // chunks)
    slot = iota((slots, rows), 0)
    for chunk in range(chunks):
        for mask in range(masks):
            row = (counts[mask : mask + 1, :] - 1 == slot) & (names[mask : mask + 1, :] > 0)
            pick = (row & (chunk_of == chunk)).astype(BF16)
            outs[chunk * masks + mask][...] = fast_dot(pick, out).astype(BF16)


def carried(prefix, received):
    states = prefix.shape[0]
    decay = received[states : states + 1, :].astype(F32)
    return prefix[...].astype(F32) * decay + received[0:states, :].astype(F32)


def grad_kernel(core, shared, prefix, received, inner, fade, b, out):
    own = carried(prefix, received)
    carry = jnp.where(core[0] != 0, shared[...].astype(F32), own)
    out[...] = inner[...] + fade[...] * fast_dot(b[...], carry.astype(BF16))


N_MASKS = 4


def norm_kernel(mine, gain, *refs):
    parts, out = refs[:-1], refs[-1]
    width = parts[0].shape[1]
    features = width * len(parts)
    values = [part[...].astype(F32) for part in parts]
    squares = sum(jnp.sum(v * v, axis=1, keepdims=True) for v in values)
    scale = lax.rsqrt(squares / features + EPSILON)
    per_half = len(parts) // 2
    for mask, value in enumerate(values):
        at = mine[0] ^ mask
        to = pl.multiple_of((at % per_half) * width, width)
        gains = gain[:, pl.ds(pl.multiple_of(at * width, width), width)]
        out[at // per_half, :, pl.ds(to, width)] = (value * scale * gains).astype(BF16)


def onward_kernel(along_x, along_y, own, to_x, to_y):
    to_x[0] = along_y[0]
    to_y[0] = along_x[1]
    to_x[1:] = own[...]
    to_y[1:] = own[...]


def arrive_kernel(from_x, from_y, far, along_x, along_y):
    far[0] = from_x[0]
    far[1] = from_y[0]
    along_x[...] = from_x[1:]
    along_y[...] = from_y[1:]


def join_kernel(from_x, from_y, far):
    far[0] = from_x[0]
    far[1] = from_y[0]


def expert_kernel(n, *refs):
    blocks, (up, down), outs, (rows_in, hidden) = refs[: 2 * n], refs[2 * n : 2 * n + 2], refs[2 * n + 2 : -2], refs[-2:]
    _, slots, half = blocks[0].shape
    for k, block in enumerate(blocks):
        rows = slice(k * slots, (k + 1) * slots)
        rows_in[rows, :half] = block[0]
        rows_in[rows, half:] = block[1]
    for j in range(0, hidden.shape[1], UP_TILE):
        value = fast_dot(rows_in[...], up[:, j : j + UP_TILE])
        hidden[:, j : j + UP_TILE] = (value * jax.nn.sigmoid(value)).astype(BF16)
    for j in range(0, down.shape[1], DOWN_TILE):
        value = fast_dot(hidden[...], down[:, j : j + DOWN_TILE]).astype(BF16)
        at = slice(j % half, j % half + DOWN_TILE)
        for k, out in enumerate(outs):
            start = (n + k) % (2 * n) * slots
            out[j // half, :, at] = value[start : start + slots]


UP_TILE = 512
DOWN_TILE = 512


def expert_rows(blocks, twins, up, down):
    n = len(blocks)
    _, slots, half = blocks[0].shape
    features, hidden = up.shape
    outs = call(
        lambda *refs: expert_kernel(n, *refs),
        [shape_of((2, slots, half), BF16)] * (2 * n),
        scratch=[pltpu.VMEM((2 * n * slots, features), BF16), pltpu.VMEM((2 * n * slots, hidden), BF16)],
        limit=8,
    )(*blocks, *twins, up, down)
    return outs[:n], outs[n:]


def both(a, b):
    return (a.astype(F32) + b.astype(F32)).astype(BF16)


def sum_over_chip(places, others, own, to_x, to_y, rest_x, rest_y):
    here, along_x, along_y, far = zip(places, others)
    own[...] = both(here[0][...], here[1][...])
    to_x[1] = both(far[0][0], far[1][0])
    to_y[1] = both(far[0][1], far[1][1])
    to_x[2] = both(along_x[0][0], along_x[1][0])
    to_y[2] = both(along_y[0][1], along_y[1][1])
    rest_x[...] = both(along_x[0][1], along_x[1][1])
    rest_y[...] = both(along_y[0][0], along_y[1][0])


def first_sum_kernel(from_x, from_y, *refs):
    places, others, outs = refs[:4], refs[4:8], refs[8:]
    outs[1][0] = from_y[1]
    outs[2][0] = from_x[2]
    sum_over_chip(places, others, *outs)


def second_sum_kernel(from_x, from_y, rest_x, rest_y, *refs):
    places, others, outs = refs[:4], refs[4:8], refs[8:]
    outs[1][0] = both(rest_x[...], from_y[1])
    outs[2][0] = both(rest_y[...], from_x[1])
    sum_over_chip(places, others, *outs)


def relay_kernel(from_x, from_y, rest_x, rest_y, next_x, next_y):
    next_x[...] = both(rest_x[...], from_y[1])
    next_y[...] = both(rest_y[...], from_x[1])


def total_kernel(at_last, mine, own, from_x, from_y, last_x, last_y, *refs):
    outs, total = refs[:-1], refs[-1]
    width = outs[0].shape[1]
    per_half = len(outs) // 2

    def add(a, b, c):
        return (a.astype(F32) + b.astype(F32) + c.astype(F32)).astype(BF16)

    total[0] = add(own[0], from_x[2], last_y[at_last])
    total[1] = add(own[1], last_x[at_last], from_y[2])
    for mask, out in enumerate(outs):
        at = mine[0] ^ mask
        to = pl.multiple_of((at % per_half) * width, width)
        out[...] = total[at // per_half, :, pl.ds(to, width)]


def combine_kernel(chunk, mine, ids, weights, *refs):
    parts, out = refs[:N_MASKS], refs[-1]
    earlier = refs[N_MASKS:-1]
    slots = parts[0].shape[0]
    rows = ids.shape[1]
    share = rows // CHUNKS
    here = slice(chunk * share, (chunk + 1) * share)
    chosen = ids[...]
    names, counts = choices(chosen, mine[0], N_MASKS, rows, CHUNKS)
    slot = iota((slots, rows), 0)
    values = jnp.concatenate([part[...] for part in parts], axis=0)
    columns = jnp.concatenate([weights[...], jnp.zeros((8 - TOPK, rows), F32)], axis=0).T
    result = jnp.zeros((share, values.shape[1]), F32)
    for k in range(TOPK):
        picks = []
        for mask in range(N_MASKS):
            row = (counts[mask : mask + 1, :] - 1 == slot) & (chosen[k : k + 1, :] == mine[0] ^ mask)
            picks.append(row.astype(F32))
        pick = jnp.concatenate(picks, axis=0).T[here].astype(BF16)
        result = result + columns[here, k : k + 1] * fast_dot(pick, values)
    result = result.astype(BF16)
    if earlier:
        out[:share] = earlier[0][...]
        out[share:] = result
    else:
        out[...] = result


def directed(x, mask):
    size = lax.axis_size("ctx")
    route = []
    for i in range(size):
        j = i ^ mask
        if (j > i) == (i % 2 == 1):
            route.append((i, j))
    return lax.ppermute(x, "ctx", route)


def exchange_shards(
    conv_input,
    conv_weight,
    b_proj,
    c_proj,
    log_decay,
    skip_gain,
    grad_in,
    norm_gain,
    expert_ids,
    expert_weights,
    up_weight,
    down_weight,
):
    rows, lanes = conv_input.shape
    heads = log_decay.shape[0]
    states = b_proj.shape[1]
    experts = lax.axis_size("exp")
    features = lanes * experts
    place = lax.axis_index("ctx")
    core = (place & 1).reshape(1)
    chip = place >> 1
    mine = lax.axis_index("exp").reshape(1)
    block = shape_of((rows, lanes), F32)
    payload = shape_of((states + DECAY_ROWS, lanes), BF16)
    slots = 3 * TOPK * rows // (2 * experts * CHUNKS)
    half = features // 2
    row_block = shape_of((2, slots, half), BF16)
    half_block = shape_of((slots, half), BF16)

    flip = jnp.where(place & 1 == 1, chip == 2, chip == 1).astype(jnp.int32).reshape(1)
    edge, core, mine, flip = lax.optimization_barrier((conv_input[rows - RIM :], core, mine, flip))
    rim = passed_along(edge, "ctx", 1)
    params = [
        after(log_decay, edge, core, mine, flip),
        c_proj,
        grad_in,
        b_proj,
        conv_input,
        conv_weight,
        skip_gain.reshape(1, heads),
        norm_gain.reshape(1, features),
        expert_ids.T,
        expert_weights.T,
    ]
    prepared = pl.pallas_call(
        lambda *refs: prepare_kernel(len(params), *refs),
        in_specs=[pl.BlockSpec(memory_space=pltpu.HBM)] * len(params),
        out_specs=[pl.BlockSpec(memory_space=pltpu.VMEM)] * (len(params) + 4),
        out_shape=[pltpu.VMEM(p.shape, p.dtype) for p in params]
        + [block, block, shape_of((states, lanes), BF16), shape_of((DECAY_ROWS, lanes), BF16)],
        scratch_shapes=[pltpu.SemaphoreType.DMA((len(params),))],
        cost_estimate=LIGHT,
        compiler_params=pltpu.CompilerParams(vmem_limit_bytes=6 << 20),
    )(*(pltpu.with_memory_space_constraint(p, pltpu.HBM) for p in params))
    decay, c, grad, b, conv, taps, skip, gain, ids, weights, grow, fade, backward, through = prepared
    mixed, sent, kept = call(
        mix_kernel, [shape_of((rows, lanes), BF16), payload, payload], smem=1
    )(core, conv, rim, taps, b, fade, backward, through)
    received = swap(sent, "ctx", 1)
    inner, grad_inner = call(inner_kernel, [block, block])(mixed, b, c, decay, grad, skip)
    chip_sum = call(pair_kernel, payload)(received, after(kept, inner))
    up = load(after(up_weight[0], chip_sum), 1)
    near, middle, far = (directed(chip_sum, mask) for mask in (2, 4, 6))
    prefix = call(reach_kernel, shape_of((states, lanes), BF16), smem=1)(
        after(flip, up), near, middle, far
    )
    shared = swap(prefix, "ctx", 1)
    picked = call(carry_kernel, [shape_of((slots, lanes), BF16)] * (CHUNKS * experts), smem=2)(
        core, mine, shared, prefix, received, inner, grow, c, ids
    )
    down = load(after(down_weight[0], picked[0]), 1)
    masks = (2, 3, 1)

    def to_experts(chunk):
        parts = picked[chunk * experts : (chunk + 1) * experts]
        arrived = {m: swap(parts[m], "exp", m) for m in masks}
        return [parts[0]] + [arrived[m] for m in range(1, experts)]

    def twin(x):
        return swap(x, "ctx", 1)

    def along(to_x, to_y):
        return swap(to_x, "ctx", 2), swap(to_y, "ctx", 4)

    def results(at_last, *sums):
        return call(
            lambda *refs: total_kernel(at_last, *refs),
            [shape_of((slots, lanes), BF16)] * experts,
            smem=1,
            scratch=[pltpu.VMEM((2, slots, half), BF16)],
        )(mine, *sums)

    def normed(arrived):
        return call(norm_kernel, row_block, smem=1)(mine, gain, *arrived)

    def back(parts):
        arrived = {m: swap(parts[m], "exp", m) for m in masks}
        return [parts[0]] + [arrived[m] for m in range(1, experts)]

    onward = shape_of((3, slots, half), BF16)
    sums = [row_block, onward, onward, half_block, half_block]
    share = rows // CHUNKS
    first1, *others1 = to_experts(0)
    own1 = normed([after(first1, down), *others1])
    x1, y1 = along(own1, own1)
    own2 = normed(to_experts(1))
    from_x, from_y = along(*call(onward_kernel, [onward, onward])(x1, y1, own2))
    near1 = [own1, x1, y1]
    odd1, even1 = expert_rows(near1, [twin(block) for block in near1], up, down)
    far1, x2, y2 = call(arrive_kernel, [row_block] * 3)(after(from_x, even1[0]), from_y)
    odd_far1, even_far1 = expert_rows([far1], [twin(far1)], up, down)
    own_sum1, to_x, to_y, rest_x1, rest_y1 = call(first_sum_kernel, sums)(
        from_x, from_y, *even1, *even_far1, *(twin(block) for block in (*odd1, *odd_far1))
    )
    from_x3, from_y3 = along(to_x, to_y)
    near2 = [own2, x2, y2]
    odd2, even2 = expert_rows(
        [after(own2, own_sum1), x2, y2], [twin(block) for block in near2], up, down
    )
    far2 = call(join_kernel, row_block)(after(from_x3, even2[0]), from_y3)
    odd_far2, even_far2 = expert_rows([far2], [twin(far2)], up, down)
    own_sum2, to_x, to_y, rest_x2, rest_y2 = call(second_sum_kernel, sums)(
        from_x3, from_y3, rest_x1, rest_y1,
        *even2, *even_far2, *(twin(block) for block in (*odd2, *odd_far2)),
    )
    from_x4, from_y4 = along(to_x, to_y)
    next_x, next_y = call(relay_kernel, [half_block, half_block])(from_x4, from_y4, rest_x2, rest_y2)
    done1 = results(0, own_sum1, from_x3, from_y3, after(from_x4, next_x), from_y4)
    last_x, last_y = along(next_x, next_y)
    back1 = back(done1)
    grad_conv = call(grad_kernel, block, smem=1)(
        core, shared, after(prefix, done1[0]), received, grad_inner, fade, b
    )
    done2 = results(slice(None), after(own_sum2, grad_conv), from_x4, from_y4, last_x, last_y)
    combined = call(
        lambda *refs: combine_kernel(0, *refs), shape_of((share, lanes), BF16), smem=1
    )(mine, after(ids, done2[0]), weights, *back1)
    moe_out = call(lambda *refs: combine_kernel(1, *refs), shape_of((rows, lanes), BF16), smem=1)(
        mine, ids, weights, *back(done2), combined
    )
    return (moe_out, grad_conv)


def solution(mesh):
    placed = (
        P("ctx", "exp"),
        P(None, "exp"),
        P("ctx", None),
        P("ctx", None),
        P("exp", "ctx"),
        P("exp"),
        P("ctx", "exp"),
        P(),
        P("ctx", None),
        P("ctx", None),
        P("exp", None, "ctx"),
        P("exp", "ctx", None),
    )
    swaps = mesh.shape["ctx"] == 8 and mesh.shape["exp"] == 4
    return jax.shard_map(
        exchange_shards if swaps else general_shards,
        mesh=mesh,
        in_specs=placed,
        out_specs=(P("ctx", "exp"), P("ctx", "exp")),
        check_vma=False,
    )
```

```python
import jax
import jax.numpy as jnp
from jax import lax
from jax.experimental import pallas as pl
from jax.experimental.pallas import tpu as pltpu
from jax.sharding import PartitionSpec as P

CONV = 4
TOPK = 2


HIGHEST = lax.Precision.HIGHEST
EPSILON = 1e-06


def passed_along(block, axis, distance):
    devices = range(lax.axis_size(axis))
    route = [(i - distance, i) for i in devices if i - distance in devices]
    return lax.ppermute(block, axis, route)


def prefix(x, axis, combine, identity, reverse):
    size, mine = (lax.axis_size(axis), lax.axis_index(axis))
    everything = jax.tree.map(
        lambda part, kind: lax.all_gather(part.astype(kind), axis), x, (jnp.bfloat16, jnp.bfloat16)
    )
    start = jax.tree.map(
        lambda part, zero: jnp.broadcast_to(jnp.asarray(zero, part.dtype), part.shape), x, identity
    )

    def turn(k, before):
        at = size - 1 - k if reverse else k
        reached = at > mine if reverse else at < mine
        new = combine(
            before, jax.tree.map(lambda part, own: part[at].astype(own.dtype), everything, x)
        )
        return jax.tree.map(lambda a, b: jnp.where(reached, a, b), new, before)

    return lax.fori_loop(0, size, turn, start)


def combine_state(earlier, later):
    return (earlier[0] * later[0], later[0][:, None, None] * earlier[1] + later[1])


def conv_mix(extended, conv_weight):
    rows_out = extended.shape[0] - conv_weight.shape[0] + 1
    total = jnp.zeros((rows_out, extended.shape[1]), jnp.float32)
    for offset in range(conv_weight.shape[0]):
        total = total + conv_weight[offset][None, :] * extended[offset : offset + rows_out]
    return jax.nn.silu(total).astype(jnp.bfloat16)


def block_terms(decay_block, b_raw, c_raw):
    totals = jnp.cumsum(decay_block, axis=1)
    rows_here = totals.shape[1]
    causal = jnp.arange(rows_here)[:, None] >= jnp.arange(rows_here)[None, :]
    spread = jnp.where(causal[None], totals[:, :, None] - totals[:, None, :], 0.0)
    kernel = (
        jnp.where(causal[None], jnp.exp(spread), 0.0)
        * jnp.dot(c_raw, b_raw.T, preferred_element_type=jnp.float32)[None]
    )
    to_end = jnp.exp(totals[:, -1:] - totals)
    return (totals, kernel, to_end)


def normalize(rows_in, norm_gain):
    values = rows_in.astype(jnp.float32)
    scale = lax.rsqrt(jnp.mean(values * values, axis=1, keepdims=True) + EPSILON)
    return (values * scale * norm_gain[None, :]).astype(jnp.bfloat16)


def route_matrix(chosen_ids, slots_each, experts):
    pairs = chosen_ids.reshape(-1)
    onehot = (pairs[:, None] == jnp.arange(experts, dtype=jnp.int32)[None, :]).astype(jnp.int32)
    ranks = jnp.sum((jnp.cumsum(onehot, axis=0) - 1) * onehot, axis=1)
    target = pairs * slots_each + ranks
    return (jnp.arange(experts * slots_each, dtype=jnp.int32)[:, None] == target[None, :]).astype(
        jnp.bfloat16
    )


def gather_back(dispatch, returned, weights):
    values = jnp.einsum("sp,sc->pc", dispatch, returned, preferred_element_type=jnp.float32)
    values = values.reshape(weights.shape[0], weights.shape[1], returned.shape[1])
    return jnp.sum(weights[:, :, None] * values, axis=1).astype(jnp.bfloat16)


def expert_block(rows_in, up_weight, down_weight):
    up_local = up_weight[0]
    down_local = down_weight[0]
    hidden = jax.nn.silu(
        jnp.dot(
            lax.all_gather(rows_in, "ctx", axis=0, tiled=True),
            up_local,
            preferred_element_type=jnp.float32,
        )
    ).astype(jnp.bfloat16)
    summed = lax.psum_scatter(
        jnp.dot(hidden, down_local, preferred_element_type=jnp.float32).astype(jnp.bfloat16),
        "ctx",
        scatter_dimension=0,
        tiled=True,
    )
    return summed


def general_shards(
    conv_input,
    conv_weight,
    b_proj,
    c_proj,
    log_decay,
    skip_gain,
    grad_in,
    norm_gain,
    expert_ids,
    expert_weights,
    up_weight,
    down_weight,
):
    tok_rows = conv_input.shape[0]
    heads_here = log_decay.shape[0]
    head_size = conv_input.shape[1] // heads_here
    rim_rows = passed_along(conv_input[tok_rows - (CONV - 1) :], "ctx", 1)
    extended = jnp.concatenate(
        [rim_rows.astype(jnp.float32), conv_input.astype(jnp.float32)], axis=0
    )
    mixed_in = conv_mix(extended, conv_weight)
    inputs_block = mixed_in.astype(jnp.float32).reshape(tok_rows, heads_here, head_size)
    b_block = b_proj.astype(jnp.float32)
    c_block = c_proj.astype(jnp.float32)
    grad_block = grad_in.astype(jnp.float32).reshape(tok_rows, heads_here, head_size)
    totals, kernel, to_end = block_terms(log_decay, b_proj, c_proj)
    through = jnp.exp(totals[:, -1])
    local_state = jnp.einsum("hs,shp,sn->hpn", to_end, inputs_block, b_block, precision=HIGHEST)
    local_grad = jnp.einsum(
        "ht,thp,tn->hpn", jnp.exp(totals), grad_block, c_block, precision=HIGHEST
    )
    zero_state = jnp.zeros_like(local_state)
    ones_heads = jnp.ones_like(through)
    carry_state = prefix(
        (through, local_state), "ctx", combine_state, (ones_heads, zero_state), False
    )[1]
    carry_grad = prefix(
        (through, local_grad), "ctx", combine_state, (ones_heads, zero_state), True
    )[1]
    inner = jnp.einsum("hts,shp->thp", kernel, inputs_block, precision=HIGHEST)
    carried = jnp.exp(totals).T[:, :, None] * jnp.einsum(
        "hpn,tn->thp", carry_state, c_block, precision=HIGHEST
    )
    output = inner + carried + skip_gain[None, :, None] * inputs_block
    ssd_out = output.reshape(tok_rows, heads_here * head_size).astype(jnp.bfloat16)
    grad_inner = jnp.einsum("hts,thp->shp", kernel, grad_block, precision=HIGHEST)
    grad_carried = to_end.T[:, :, None] * jnp.einsum(
        "hpn,sn->shp", carry_grad, b_block, precision=HIGHEST
    )
    grad_conv = (grad_inner + grad_carried + skip_gain[None, :, None] * grad_block).reshape(
        tok_rows, heads_here * head_size
    )
    experts = lax.axis_size("exp")
    most_rows = 3 * TOPK * tok_rows // (2 * experts * experts)
    share = tok_rows // experts
    token_view = lax.all_to_all(ssd_out, "exp", split_axis=0, concat_axis=1, tiled=True)
    normed = normalize(token_view, norm_gain)
    first_row = lax.axis_index("exp") * share
    my_ids = lax.dynamic_slice_in_dim(expert_ids, first_row, share, 0)
    my_weights = lax.dynamic_slice_in_dim(expert_weights, first_row, share, 0)
    dispatch = route_matrix(my_ids, most_rows, experts)
    outgoing = jnp.dot(
        dispatch, jnp.repeat(normed, TOPK, axis=0), preferred_element_type=jnp.float32
    ).astype(jnp.bfloat16)
    incoming = lax.all_to_all(
        outgoing.reshape(experts, most_rows, normed.shape[1]),
        "exp",
        split_axis=0,
        concat_axis=0,
        tiled=True,
    )
    results = expert_block(
        incoming.reshape(experts * most_rows, normed.shape[1]), up_weight, down_weight
    )
    returned = lax.all_to_all(
        results.reshape(experts, most_rows, normed.shape[1]),
        "exp",
        split_axis=0,
        concat_axis=0,
        tiled=True,
    )
    combined = gather_back(
        dispatch, returned.reshape(experts * most_rows, normed.shape[1]), my_weights
    )
    moe_out = lax.all_to_all(combined, "exp", split_axis=1, concat_axis=0, tiled=True)
    return (moe_out, grad_conv)


CHUNKS = 2
LIGHT = pl.CostEstimate(flops=1, transcendentals=0, bytes_accessed=1)
DECAY_ROWS = 8
RIM = 8
F32 = jnp.float32
BF16 = jnp.bfloat16


def shape_of(shape, dtype):
    return jax.ShapeDtypeStruct(shape, dtype)


def call(body, outs, smem=0, scratch=(), limit=6):
    def run(*args):
        specs = [pl.BlockSpec(memory_space=pltpu.SMEM)] * smem
        specs += [pl.BlockSpec(memory_space=pltpu.VMEM)] * (len(args) - smem)
        return pl.pallas_call(
            body,
            out_shape=outs,
            in_specs=specs,
            out_specs=jax.tree.map(lambda _: pl.BlockSpec(memory_space=pltpu.VMEM), outs),
            scratch_shapes=scratch,
            cost_estimate=LIGHT,
            compiler_params=pltpu.CompilerParams(vmem_limit_bytes=limit << 20),
        )(*args)

    return run


def swap(x, axis, mask):
    size = lax.axis_size(axis)
    return lax.ppermute(x, axis, [(i, i ^ mask) for i in range(size)])


def exact_dot(a, b, dims=(((1,), (0,)), ((), ()))):
    return lax.dot_general(a, b, dims, precision=HIGHEST, preferred_element_type=F32)


def fast_dot(a, b):
    return jnp.dot(a, b, preferred_element_type=F32)


def iota(shape, dim):
    return lax.broadcasted_iota(jnp.int32, shape, dim)


def decay_columns(decay):
    rows = decay.shape[1]
    tri = (iota((rows, rows), 0) >= iota((rows, rows), 1)).astype(F32)
    return exact_dot(tri, decay, (((1,), (1,)), ((), ())))


def prepare_kernel(n, *refs):
    sources, held = refs[:n], refs[n : 2 * n]
    grow, fade, backward, through, sems = refs[2 * n :]
    copies = [pltpu.make_async_copy(a, b, sems.at[k]) for k, (a, b) in enumerate(zip(sources, held))]
    for copy in copies:
        copy.start()
    for copy in copies:
        copy.wait()
    decay, c, grad = held[:3]
    heads = decay.shape[0]
    rows, lanes = grad.shape
    columns = decay_columns(decay[...])
    width = lanes // heads
    spread = (iota((heads, lanes), 1) // width == iota((heads, lanes), 0)).astype(F32)
    totals = exact_dot(columns, spread)
    last = totals[rows - 1 : rows, :]
    growing = jnp.exp(totals)
    grow[...] = growing
    fade[...] = jnp.exp(last - totals)
    through[...] = jnp.broadcast_to(jnp.exp(last), (DECAY_ROWS, lanes)).astype(BF16)
    backward[...] = fast_dot(c[...].T, (growing * grad[...].astype(F32)).astype(BF16)).astype(BF16)


def mix_kernel(core, conv, rim, taps, b, fade, backward, through, mixed_out, sent, kept):
    rows, lanes = conv.shape
    x = conv[...].astype(F32)
    extended = jnp.concatenate([rim[...].astype(F32), x], axis=0)
    total = jnp.zeros((rows, lanes), F32)
    for tap in range(CONV):
        start = RIM - (CONV - 1) + tap
        total = total + taps[tap : tap + 1, :] * extended[start : start + rows]
    mixed = (total * jax.nn.sigmoid(total)).astype(BF16)
    mixed_out[...] = mixed
    states = b.shape[1]
    forward = fast_dot(b[...].T, (fade[...] * mixed.astype(F32)).astype(BF16)).astype(BF16)
    first = core[0] == 0
    sent[0:states, :] = jnp.where(first, forward, backward[...])
    kept[0:states, :] = jnp.where(first, backward[...], forward)
    sent[states:, :] = through[...]
    kept[states:, :] = through[...]


def load_kernel(source, held, sem):
    copy = pltpu.make_async_copy(source, held, sem)
    copy.start()
    copy.wait()


def load(source, limit):
    return pl.pallas_call(
        load_kernel,
        out_shape=pltpu.VMEM(source.shape, source.dtype),
        in_specs=[pl.BlockSpec(memory_space=pltpu.HBM)],
        out_specs=pl.BlockSpec(memory_space=pltpu.VMEM),
        scratch_shapes=[pltpu.SemaphoreType.DMA],
        cost_estimate=LIGHT,
        compiler_params=pltpu.CompilerParams(vmem_limit_bytes=limit << 20),
    )(pltpu.with_memory_space_constraint(source, pltpu.HBM))


def after(x, *others):
    return lax.optimization_barrier((x, *others))[0]


def pair_kernel(received, kept, chip):
    states = kept.shape[0] - DECAY_ROWS
    decay = kept[states : states + 1, :].astype(F32)
    got = received[0:states, :].astype(F32)
    chip[0:states, :] = (got * decay + kept[0:states, :].astype(F32)).astype(BF16)
    both = decay * received[states : states + 1, :].astype(F32)
    chip[states:, :] = jnp.broadcast_to(both, (DECAY_ROWS, both.shape[1])).astype(BF16)


def reach_kernel(flip, near, middle, far, mine):
    states = mine.shape[0]
    flipped = flip[0] != 0

    def part(ref):
        return ref[0:states, :].astype(F32), ref[states : states + 1, :].astype(F32)

    a, a_decay = part(near)
    b, b_decay = part(middle)
    c, c_decay = part(far)
    first, first_decay = jnp.where(flipped, c, a), jnp.where(flipped, c_decay, a_decay)
    third = jnp.where(flipped, a, c)
    mine[...] = (first + first_decay * (b + b_decay * third)).astype(BF16)


def inner_kernel(mixed, b, c, decay, grad, skip, out, grad_out):
    heads, rows = decay.shape
    lanes = mixed.shape[1]
    width = lanes // heads
    pack = 128 // width
    columns = decay_columns(decay[...])
    tri_rows = (iota((rows, rows), 0) <= iota((rows, rows), 1)).astype(F32)
    totals = exact_dot(decay[...], tri_rows)
    nt = (((1,), (1,)), ((), ()))
    scores = lax.dot_general(c[...], b[...], nt, preferred_element_type=F32)
    flipped = lax.dot_general(b[...], c[...], nt, preferred_element_type=F32)
    t, s = iota((rows, rows), 0), iota((rows, rows), 1)
    spread = (iota((heads, lanes), 1) // width == iota((heads, lanes), 0)).astype(F32)
    gains = exact_dot(skip[...], spread)
    lane = iota((rows, 128), 1) // width
    for group in range(lanes // 128):
        at = slice(group * 128, group * 128 + 128)
        x = mixed[:, at]
        g = grad[:, at]
        left, right, xs, gs = [], [], [], []
        for k in range(pack):
            h = group * pack + k
            gap = columns[:, h : h + 1] - totals[h : h + 1, :]
            left.append((jnp.exp(jnp.where(t >= s, gap, -1e30)) * scores).astype(BF16))
            right.append((jnp.exp(jnp.where(t <= s, -gap, -1e30)) * flipped).astype(BF16))
            xs.append(jnp.where(lane == k, x, jnp.zeros_like(x)))
            gs.append(jnp.where(lane == k, g, jnp.zeros_like(g)))
        gain = gains[0:1, at]
        out[:, at] = fast_dot(jnp.concatenate(left, 1), jnp.concatenate(xs, 0)) + gain * x.astype(F32)
        grad_out[:, at] = fast_dot(jnp.concatenate(right, 1), jnp.concatenate(gs, 0)) + gain * g.astype(F32)


def choices(ids, mine, masks, rows, chunks):
    named = []
    for mask in range(masks):
        wanted = mine ^ mask
        named.append(((ids[0:1, :] == wanted) | (ids[1:2, :] == wanted)).astype(F32))
    named.append(jnp.zeros((8 - masks, rows), F32))
    names = jnp.concatenate(named, axis=0)
    before, after = iota((rows, rows), 0), iota((rows, rows), 1)
    share = rows // chunks
    tri = ((before <= after) & (before // share == after // share)).astype(BF16)
    return names, fast_dot(names.astype(BF16), tri).astype(jnp.int32)


def carry_kernel(core, mine, shared, prefix, received, inner, grow, c, ids, *outs):
    chunks, masks = len(outs) // N_MASKS, N_MASKS
    states, lanes = prefix.shape
    rows = inner.shape[0]
    own = carried(prefix, received)
    carry = jnp.where(core[0] != 0, own, shared[...].astype(F32))
    out = inner[...] + grow[...] * fast_dot(c[...], carry.astype(BF16))
    out = out.astype(BF16)
    names, counts = choices(ids[...], mine[0], masks, rows, chunks)
    slots = outs[0].shape[0]
    chunk_of = iota((slots, rows), 1) // (rows // chunks)
    slot = iota((slots, rows), 0)
    for chunk in range(chunks):
        for mask in range(masks):
            row = (counts[mask : mask + 1, :] - 1 == slot) & (names[mask : mask + 1, :] > 0)
            pick = (row & (chunk_of == chunk)).astype(BF16)
            outs[chunk * masks + mask][...] = fast_dot(pick, out).astype(BF16)


def carried(prefix, received):
    states = prefix.shape[0]
    decay = received[states : states + 1, :].astype(F32)
    return prefix[...].astype(F32) * decay + received[0:states, :].astype(F32)


def grad_kernel(core, shared, prefix, received, inner, fade, b, out):
    own = carried(prefix, received)
    carry = jnp.where(core[0] != 0, shared[...].astype(F32), own)
    out[...] = inner[...] + fade[...] * fast_dot(b[...], carry.astype(BF16))


N_MASKS = 4


def norm_kernel(mine, gain, *refs):
    parts, out = refs[:-1], refs[-1]
    width = parts[0].shape[1]
    features = width * len(parts)
    values = [part[...].astype(F32) for part in parts]
    squares = sum(jnp.sum(v * v, axis=1, keepdims=True) for v in values)
    scale = lax.rsqrt(squares / features + EPSILON)
    per_half = len(parts) // 2
    for mask, value in enumerate(values):
        at = mine[0] ^ mask
        to = pl.multiple_of((at % per_half) * width, width)
        gains = gain[:, pl.ds(pl.multiple_of(at * width, width), width)]
        out[at // per_half, :, pl.ds(to, width)] = (value * scale * gains).astype(BF16)


def onward_kernel(along_x, along_y, own, to_x, to_y):
    to_x[0] = along_y[0]
    to_y[0] = along_x[1]
    to_x[1:] = own[...]
    to_y[1:] = own[...]


def join_kernel(from_x, from_y, far):
    far[0] = from_x[0]
    far[1] = from_y[0]


def expert_kernel(n, n_split, *refs):
    blocks, (up, down), outs, (rows_in, hidden) = refs[: 2 * n], refs[2 * n : 2 * n + 2], refs[2 * n + 2 : -2], refs[-2:]
    _, slots, half = blocks[0].shape
    for k, block in enumerate(blocks):
        rows = slice(k * slots, (k + 1) * slots)
        rows_in[rows, :half] = block[0]
        rows_in[rows, half:] = block[1]
    for j in range(0, hidden.shape[1], UP_TILE):
        value = fast_dot(rows_in[...], up[:, j : j + UP_TILE])
        hidden[:, j : j + UP_TILE] = (value * jax.nn.sigmoid(value)).astype(BF16)
    for j in range(0, down.shape[1], DOWN_TILE):
        value = fast_dot(hidden[...], down[:, j : j + DOWN_TILE]).astype(BF16)
        at = slice(j % half, j % half + DOWN_TILE)
        for k in range(2 * n):
            start = (n + k) % (2 * n) * slots
            rows = value[start : start + slots]
            if k < n_split:
                outs[2 * k + j // half][:, at] = rows
            else:
                outs[n_split + k][j // half, :, at] = rows


UP_TILE = 512
DOWN_TILE = 512


def expert_rows(blocks, twins, up, down, n_split=0):
    n = len(blocks)
    _, slots, half = blocks[0].shape
    features, hidden = up.shape
    whole, part = shape_of((2, slots, half), BF16), shape_of((slots, half), BF16)
    outs = call(
        lambda *refs: expert_kernel(n, n_split, *refs),
        [part] * (2 * n_split) + [whole] * (2 * n - n_split),
        scratch=[pltpu.VMEM((2 * n * slots, features), BF16), pltpu.VMEM((2 * n * slots, hidden), BF16)],
        limit=9,
    )(*blocks, *twins, up, down)
    return outs[: n + n_split], outs[n + n_split :]


def both(a, b):
    return (a.astype(F32) + b.astype(F32)).astype(BF16)


def arrive_kernel(from_x, from_y, *refs):
    places, others, (far, along_x, along_y, own, to_x, to_y, rest_x, rest_y) = refs[:3], refs[3:6], refs[6:]
    far[0] = from_x[0]
    far[1] = from_y[0]
    along_x[...] = from_x[1:]
    along_y[...] = from_y[1:]
    to_x[0] = from_y[1]
    to_y[0] = from_x[2]
    direct_sums(places, others, own, to_x.at[1], to_y.at[1], rest_x, rest_y)


def direct_sums(places, others, own, to_x, to_y, rest_x, rest_y):
    here, along_x, along_y = zip(places, others)
    own[...] = both(here[0][...], here[1][...])
    to_x[...] = both(along_x[0][0], along_x[1][0])
    to_y[...] = both(along_y[0][1], along_y[1][1])
    rest_x[...] = both(along_x[0][1], along_x[1][1])
    rest_y[...] = both(along_y[0][0], along_y[1][0])


def middle_kernel(far, far_other, *refs):
    places, others, (own, to_x, to_y, rest_x, rest_y) = refs[:3], refs[3:6], refs[6:]
    to_x[0] = both(far[0], far_other[0])
    to_y[0] = both(far[1], far_other[1])
    direct_sums(places, others, own, to_x.at[1], to_y.at[1], rest_x, rest_y)


def late_kernel(from_x, from_y, rest_x, rest_y, far, first_half, second_half, to_x, to_y):
    to_x[0] = both(rest_x[...], from_y[0])
    to_y[0] = both(rest_y[...], from_x[0])
    to_x[1] = both(far[0], first_half[...])
    to_y[1] = both(far[1], second_half[...])


def relay_kernel(from_x, from_y, rest_x, rest_y, next_x, next_y):
    next_x[...] = both(rest_x[...], from_y[1])
    next_y[...] = both(rest_y[...], from_x[1])


def total_kernel(at_last, mine, own, from_x, from_y, last_x, last_y, *refs):
    outs, total = refs[:-1], refs[-1]
    width = outs[0].shape[1]
    per_half = len(outs) // 2

    def add(a, b, c):
        return (a.astype(F32) + b.astype(F32) + c.astype(F32)).astype(BF16)

    total[0] = add(own[0], from_x[1], last_y[at_last])
    total[1] = add(own[1], last_x[at_last], from_y[1])
    for mask, out in enumerate(outs):
        at = mine[0] ^ mask
        to = pl.multiple_of((at % per_half) * width, width)
        out[...] = total[at // per_half, :, pl.ds(to, width)]


def combine_kernel(chunk, mine, ids, weights, *refs):
    parts, out = refs[:N_MASKS], refs[-1]
    earlier = refs[N_MASKS:-1]
    slots = parts[0].shape[0]
    rows = ids.shape[1]
    share = rows // CHUNKS
    here = slice(chunk * share, (chunk + 1) * share)
    chosen = ids[...]
    names, counts = choices(chosen, mine[0], N_MASKS, rows, CHUNKS)
    slot = iota((slots, rows), 0)
    values = jnp.concatenate([part[...] for part in parts], axis=0)
    columns = jnp.concatenate([weights[...], jnp.zeros((8 - TOPK, rows), F32)], axis=0).T
    result = jnp.zeros((share, values.shape[1]), F32)
    for k in range(TOPK):
        picks = []
        for mask in range(N_MASKS):
            row = (counts[mask : mask + 1, :] - 1 == slot) & (chosen[k : k + 1, :] == mine[0] ^ mask)
            picks.append(row.astype(F32))
        pick = jnp.concatenate(picks, axis=0).T[here].astype(BF16)
        result = result + columns[here, k : k + 1] * fast_dot(pick, values)
    result = result.astype(BF16)
    if earlier:
        out[:share] = earlier[0][...]
        out[share:] = result
    else:
        out[...] = result


def directed(x, mask):
    size = lax.axis_size("ctx")
    route = []
    for i in range(size):
        j = i ^ mask
        if (j > i) == (i % 2 == 1):
            route.append((i, j))
    return lax.ppermute(x, "ctx", route)


def exchange_shards(
    conv_input,
    conv_weight,
    b_proj,
    c_proj,
    log_decay,
    skip_gain,
    grad_in,
    norm_gain,
    expert_ids,
    expert_weights,
    up_weight,
    down_weight,
):
    rows, lanes = conv_input.shape
    heads = log_decay.shape[0]
    states = b_proj.shape[1]
    experts = lax.axis_size("exp")
    features = lanes * experts
    place = lax.axis_index("ctx")
    core = (place & 1).reshape(1)
    chip = place >> 1
    mine = lax.axis_index("exp").reshape(1)
    block = shape_of((rows, lanes), F32)
    payload = shape_of((states + DECAY_ROWS, lanes), BF16)
    slots = 3 * TOPK * rows // (2 * experts * CHUNKS)
    half = features // 2
    row_block = shape_of((2, slots, half), BF16)
    half_block = shape_of((slots, half), BF16)

    flip = jnp.where(place & 1 == 1, chip == 2, chip == 1).astype(jnp.int32).reshape(1)
    edge, core, mine, flip = lax.optimization_barrier((conv_input[rows - RIM :], core, mine, flip))
    rim = passed_along(edge, "ctx", 1)
    params = [
        after(log_decay, edge, core, mine, flip),
        c_proj,
        grad_in,
        b_proj,
        conv_input,
        conv_weight,
        skip_gain.reshape(1, heads),
        norm_gain.reshape(1, features),
        expert_ids.T,
        expert_weights.T,
    ]
    prepared = pl.pallas_call(
        lambda *refs: prepare_kernel(len(params), *refs),
        in_specs=[pl.BlockSpec(memory_space=pltpu.HBM)] * len(params),
        out_specs=[pl.BlockSpec(memory_space=pltpu.VMEM)] * (len(params) + 4),
        out_shape=[pltpu.VMEM(p.shape, p.dtype) for p in params]
        + [block, block, shape_of((states, lanes), BF16), shape_of((DECAY_ROWS, lanes), BF16)],
        scratch_shapes=[pltpu.SemaphoreType.DMA((len(params),))],
        cost_estimate=LIGHT,
        compiler_params=pltpu.CompilerParams(vmem_limit_bytes=6 << 20),
    )(*(pltpu.with_memory_space_constraint(p, pltpu.HBM) for p in params))
    decay, c, grad, b, conv, taps, skip, gain, ids, weights, grow, fade, backward, through = prepared
    mixed, sent, kept = call(
        mix_kernel, [shape_of((rows, lanes), BF16), payload, payload], smem=1
    )(core, conv, rim, taps, b, fade, backward, through)
    received = swap(sent, "ctx", 1)
    inner, grad_inner = call(inner_kernel, [block, block])(mixed, b, c, decay, grad, skip)
    chip_sum = call(pair_kernel, payload)(received, after(kept, inner))
    up = load(after(up_weight[0], chip_sum), 1)
    near, middle, far = (directed(chip_sum, mask) for mask in (2, 4, 6))
    prefix = call(reach_kernel, shape_of((states, lanes), BF16), smem=1)(
        after(flip, up), near, middle, far
    )
    shared = swap(prefix, "ctx", 1)
    picked = call(carry_kernel, [shape_of((slots, lanes), BF16)] * (CHUNKS * experts), smem=2)(
        core, mine, shared, prefix, received, inner, grow, c, ids
    )
    down = load(after(down_weight[0], picked[0]), 1)
    masks = (2, 3, 1)

    def to_experts(chunk):
        parts = picked[chunk * experts : (chunk + 1) * experts]
        arrived = {m: swap(parts[m], "exp", m) for m in masks}
        return [parts[0]] + [arrived[m] for m in range(1, experts)]

    def twin(x):
        return swap(x, "ctx", 1)

    def along(to_x, to_y):
        return swap(to_x, "ctx", 2), swap(to_y, "ctx", 4)

    def results(at_last, *sums):
        return call(
            lambda *refs: total_kernel(at_last, *refs),
            [shape_of((slots, lanes), BF16)] * experts,
            smem=1,
            scratch=[pltpu.VMEM((2, slots, half), BF16)],
        )(mine, *sums)

    def normed(arrived):
        return call(norm_kernel, row_block, smem=1)(mine, gain, *arrived)

    def back(parts):
        arrived = {m: swap(parts[m], "exp", m) for m in masks}
        return [parts[0]] + [arrived[m] for m in range(1, experts)]

    onward = shape_of((3, slots, half), BF16)
    share = rows // CHUNKS
    first1, *others1 = to_experts(0)
    own1 = normed([after(first1, down), *others1])
    x1, y1 = along(own1, own1)
    own2 = normed(to_experts(1))
    from_x, from_y = along(*call(onward_kernel, [onward, onward])(x1, y1, own2))
    double = shape_of((2, slots, half), BF16)
    sums = [row_block, double, double, half_block, half_block]
    now = [own1, x1, y1, own2]
    (*odd1, odd_own2), (*even1, even_own2) = expert_rows(now, [twin(block) for block in now], up, down)
    far1, x2, y2, own_sum1, to_x, to_y, rest_x1, rest_y1 = call(arrive_kernel, [row_block] * 3 + sums)(
        after(from_x, even1[0]), from_y, *even1, *(twin(block) for block in odd1)
    )
    from_x3, from_y3 = along(to_x, to_y)
    now = [far1, x2, y2]
    odd, even = expert_rows(now, [twin(block) for block in now], up, down)
    far2 = call(join_kernel, row_block)(after(from_x3, even[0]), from_y3)
    own_sum2, to_x, to_y, rest_x2, rest_y2 = call(middle_kernel, sums)(
        after(even[0], far2), twin(odd[0]),
        even_own2, *even[1:], twin(odd_own2), *(twin(block) for block in odd[1:]),
    )
    from_x4, from_y4 = along(to_x, to_y)
    odd_far2, (even_far2,) = expert_rows(
        [after(far2, own_sum2)], [twin(far2)], up, down, n_split=1
    )
    to_x, to_y = call(late_kernel, [double, double])(
        from_x4, from_y4, rest_x1, rest_y1, even_far2, *(twin(part) for part in odd_far2)
    )
    from_x5, from_y5 = along(to_x, to_y)
    next_x, next_y = call(relay_kernel, [half_block, half_block])(from_x5, from_y5, rest_x2, rest_y2)
    done1 = results(0, own_sum1, from_x3, from_y3, after(from_x5, next_x), from_y5)
    last_x, last_y = along(next_x, next_y)
    back1 = back(done1)
    grad_conv = call(grad_kernel, block, smem=1)(
        core, shared, after(prefix, done1[0]), received, grad_inner, fade, b
    )
    done2 = results(slice(None), after(own_sum2, grad_conv), from_x4, from_y4, last_x, last_y)
    combined = call(
        lambda *refs: combine_kernel(0, *refs), shape_of((share, lanes), BF16), smem=1
    )(mine, after(ids, done2[0]), weights, *back1)
    moe_out = call(lambda *refs: combine_kernel(1, *refs), shape_of((rows, lanes), BF16), smem=1)(
        mine, ids, weights, *back(done2), combined
    )
    return (moe_out, grad_conv)


def solution(mesh):
    placed = (
        P("ctx", "exp"),
        P(None, "exp"),
        P("ctx", None),
        P("ctx", None),
        P("exp", "ctx"),
        P("exp"),
        P("ctx", "exp"),
        P(),
        P("ctx", None),
        P("ctx", None),
        P("exp", None, "ctx"),
        P("exp", "ctx", None),
    )
    swaps = mesh.shape["ctx"] == 8 and mesh.shape["exp"] == 4
    return jax.shard_map(
        exchange_shards if swaps else general_shards,
        mesh=mesh,
        in_specs=placed,
        out_specs=(P("ctx", "exp"), P("ctx", "exp")),
        check_vma=False,
    )
```

```python
import jax
import jax.numpy as jnp
from jax import lax
from jax.experimental import pallas as pl
from jax.experimental.pallas import tpu as pltpu
from jax.sharding import PartitionSpec as P

CONV = 4
TOPK = 2


HIGHEST = lax.Precision.HIGHEST
EPSILON = 1e-06


def passed_along(block, axis, distance):
    devices = range(lax.axis_size(axis))
    route = [(i - distance, i) for i in devices if i - distance in devices]
    return lax.ppermute(block, axis, route)


def prefix(x, axis, combine, identity, reverse):
    size, mine = (lax.axis_size(axis), lax.axis_index(axis))
    everything = jax.tree.map(
        lambda part, kind: lax.all_gather(part.astype(kind), axis), x, (jnp.bfloat16, jnp.bfloat16)
    )
    start = jax.tree.map(
        lambda part, zero: jnp.broadcast_to(jnp.asarray(zero, part.dtype), part.shape), x, identity
    )

    def turn(k, before):
        at = size - 1 - k if reverse else k
        reached = at > mine if reverse else at < mine
        new = combine(
            before, jax.tree.map(lambda part, own: part[at].astype(own.dtype), everything, x)
        )
        return jax.tree.map(lambda a, b: jnp.where(reached, a, b), new, before)

    return lax.fori_loop(0, size, turn, start)


def combine_state(earlier, later):
    return (earlier[0] * later[0], later[0][:, None, None] * earlier[1] + later[1])


def conv_mix(extended, conv_weight):
    rows_out = extended.shape[0] - conv_weight.shape[0] + 1
    total = jnp.zeros((rows_out, extended.shape[1]), jnp.float32)
    for offset in range(conv_weight.shape[0]):
        total = total + conv_weight[offset][None, :] * extended[offset : offset + rows_out]
    return jax.nn.silu(total).astype(jnp.bfloat16)


def block_terms(decay_block, b_raw, c_raw):
    totals = jnp.cumsum(decay_block, axis=1)
    rows_here = totals.shape[1]
    causal = jnp.arange(rows_here)[:, None] >= jnp.arange(rows_here)[None, :]
    spread = jnp.where(causal[None], totals[:, :, None] - totals[:, None, :], 0.0)
    kernel = (
        jnp.where(causal[None], jnp.exp(spread), 0.0)
        * jnp.dot(c_raw, b_raw.T, preferred_element_type=jnp.float32)[None]
    )
    to_end = jnp.exp(totals[:, -1:] - totals)
    return (totals, kernel, to_end)


def normalize(rows_in, norm_gain):
    values = rows_in.astype(jnp.float32)
    scale = lax.rsqrt(jnp.mean(values * values, axis=1, keepdims=True) + EPSILON)
    return (values * scale * norm_gain[None, :]).astype(jnp.bfloat16)


def route_matrix(chosen_ids, slots_each, experts):
    pairs = chosen_ids.reshape(-1)
    onehot = (pairs[:, None] == jnp.arange(experts, dtype=jnp.int32)[None, :]).astype(jnp.int32)
    ranks = jnp.sum((jnp.cumsum(onehot, axis=0) - 1) * onehot, axis=1)
    target = pairs * slots_each + ranks
    return (jnp.arange(experts * slots_each, dtype=jnp.int32)[:, None] == target[None, :]).astype(
        jnp.bfloat16
    )


def gather_back(dispatch, returned, weights):
    values = jnp.einsum("sp,sc->pc", dispatch, returned, preferred_element_type=jnp.float32)
    values = values.reshape(weights.shape[0], weights.shape[1], returned.shape[1])
    return jnp.sum(weights[:, :, None] * values, axis=1).astype(jnp.bfloat16)


def expert_block(rows_in, up_weight, down_weight):
    up_local = up_weight[0]
    down_local = down_weight[0]
    hidden = jax.nn.silu(
        jnp.dot(
            lax.all_gather(rows_in, "ctx", axis=0, tiled=True),
            up_local,
            preferred_element_type=jnp.float32,
        )
    ).astype(jnp.bfloat16)
    summed = lax.psum_scatter(
        jnp.dot(hidden, down_local, preferred_element_type=jnp.float32).astype(jnp.bfloat16),
        "ctx",
        scatter_dimension=0,
        tiled=True,
    )
    return summed


def general_shards(
    conv_input,
    conv_weight,
    b_proj,
    c_proj,
    log_decay,
    skip_gain,
    grad_in,
    norm_gain,
    expert_ids,
    expert_weights,
    up_weight,
    down_weight,
):
    tok_rows = conv_input.shape[0]
    heads_here = log_decay.shape[0]
    head_size = conv_input.shape[1] // heads_here
    rim_rows = passed_along(conv_input[tok_rows - (CONV - 1) :], "ctx", 1)
    extended = jnp.concatenate(
        [rim_rows.astype(jnp.float32), conv_input.astype(jnp.float32)], axis=0
    )
    mixed_in = conv_mix(extended, conv_weight)
    inputs_block = mixed_in.astype(jnp.float32).reshape(tok_rows, heads_here, head_size)
    b_block = b_proj.astype(jnp.float32)
    c_block = c_proj.astype(jnp.float32)
    grad_block = grad_in.astype(jnp.float32).reshape(tok_rows, heads_here, head_size)
    totals, kernel, to_end = block_terms(log_decay, b_proj, c_proj)
    through = jnp.exp(totals[:, -1])
    local_state = jnp.einsum("hs,shp,sn->hpn", to_end, inputs_block, b_block, precision=HIGHEST)
    local_grad = jnp.einsum(
        "ht,thp,tn->hpn", jnp.exp(totals), grad_block, c_block, precision=HIGHEST
    )
    zero_state = jnp.zeros_like(local_state)
    ones_heads = jnp.ones_like(through)
    carry_state = prefix(
        (through, local_state), "ctx", combine_state, (ones_heads, zero_state), False
    )[1]
    carry_grad = prefix(
        (through, local_grad), "ctx", combine_state, (ones_heads, zero_state), True
    )[1]
    inner = jnp.einsum("hts,shp->thp", kernel, inputs_block, precision=HIGHEST)
    carried = jnp.exp(totals).T[:, :, None] * jnp.einsum(
        "hpn,tn->thp", carry_state, c_block, precision=HIGHEST
    )
    output = inner + carried + skip_gain[None, :, None] * inputs_block
    ssd_out = output.reshape(tok_rows, heads_here * head_size).astype(jnp.bfloat16)
    grad_inner = jnp.einsum("hts,thp->shp", kernel, grad_block, precision=HIGHEST)
    grad_carried = to_end.T[:, :, None] * jnp.einsum(
        "hpn,sn->shp", carry_grad, b_block, precision=HIGHEST
    )
    grad_conv = (grad_inner + grad_carried + skip_gain[None, :, None] * grad_block).reshape(
        tok_rows, heads_here * head_size
    )
    experts = lax.axis_size("exp")
    most_rows = 3 * TOPK * tok_rows // (2 * experts * experts)
    share = tok_rows // experts
    token_view = lax.all_to_all(ssd_out, "exp", split_axis=0, concat_axis=1, tiled=True)
    normed = normalize(token_view, norm_gain)
    first_row = lax.axis_index("exp") * share
    my_ids = lax.dynamic_slice_in_dim(expert_ids, first_row, share, 0)
    my_weights = lax.dynamic_slice_in_dim(expert_weights, first_row, share, 0)
    dispatch = route_matrix(my_ids, most_rows, experts)
    outgoing = jnp.dot(
        dispatch, jnp.repeat(normed, TOPK, axis=0), preferred_element_type=jnp.float32
    ).astype(jnp.bfloat16)
    incoming = lax.all_to_all(
        outgoing.reshape(experts, most_rows, normed.shape[1]),
        "exp",
        split_axis=0,
        concat_axis=0,
        tiled=True,
    )
    results = expert_block(
        incoming.reshape(experts * most_rows, normed.shape[1]), up_weight, down_weight
    )
    returned = lax.all_to_all(
        results.reshape(experts, most_rows, normed.shape[1]),
        "exp",
        split_axis=0,
        concat_axis=0,
        tiled=True,
    )
    combined = gather_back(
        dispatch, returned.reshape(experts * most_rows, normed.shape[1]), my_weights
    )
    moe_out = lax.all_to_all(combined, "exp", split_axis=1, concat_axis=0, tiled=True)
    return (moe_out, grad_conv)


CHUNKS = 2
LIGHT = pl.CostEstimate(flops=1, transcendentals=0, bytes_accessed=1)
DECAY_ROWS = 8
RIM = 8
F32 = jnp.float32
BF16 = jnp.bfloat16


def shape_of(shape, dtype):
    return jax.ShapeDtypeStruct(shape, dtype)


def call(body, outs, smem=0, scratch=(), limit=6):
    def run(*args):
        specs = [pl.BlockSpec(memory_space=pltpu.SMEM)] * smem
        specs += [pl.BlockSpec(memory_space=pltpu.VMEM)] * (len(args) - smem)
        return pl.pallas_call(
            body,
            out_shape=outs,
            in_specs=specs,
            out_specs=jax.tree.map(lambda _: pl.BlockSpec(memory_space=pltpu.VMEM), outs),
            scratch_shapes=scratch,
            cost_estimate=LIGHT,
            compiler_params=pltpu.CompilerParams(vmem_limit_bytes=limit << 20),
        )(*args)

    return run


def swap(x, axis, mask):
    size = lax.axis_size(axis)
    return lax.ppermute(x, axis, [(i, i ^ mask) for i in range(size)])


def exact_dot(a, b, dims=(((1,), (0,)), ((), ()))):
    return lax.dot_general(a, b, dims, precision=HIGHEST, preferred_element_type=F32)


def fast_dot(a, b):
    return jnp.dot(a, b, preferred_element_type=F32)


def iota(shape, dim):
    return lax.broadcasted_iota(jnp.int32, shape, dim)


def decay_columns(decay):
    rows = decay.shape[1]
    tri = (iota((rows, rows), 0) >= iota((rows, rows), 1)).astype(F32)
    return exact_dot(tri, decay, (((1,), (1,)), ((), ())))


def prepare_kernel(n, *refs):
    sources, held = refs[:n], refs[n : 2 * n]
    grow, fade, backward, through, sems = refs[2 * n :]
    copies = [pltpu.make_async_copy(a, b, sems.at[k]) for k, (a, b) in enumerate(zip(sources, held))]
    for copy in copies:
        copy.start()
    for copy in copies:
        copy.wait()
    decay, c, grad = held[:3]
    heads = decay.shape[0]
    rows, lanes = grad.shape
    columns = decay_columns(decay[...])
    width = lanes // heads
    spread = (iota((heads, lanes), 1) // width == iota((heads, lanes), 0)).astype(F32)
    totals = exact_dot(columns, spread)
    last = totals[rows - 1 : rows, :]
    growing = jnp.exp(totals)
    grow[...] = growing
    fade[...] = jnp.exp(last - totals)
    through[...] = jnp.broadcast_to(jnp.exp(last), (DECAY_ROWS, lanes)).astype(BF16)
    backward[...] = fast_dot(c[...].T, (growing * grad[...].astype(F32)).astype(BF16)).astype(BF16)


def mix_kernel(core, conv, rim, taps, b, fade, backward, through, mixed_out, sent, kept):
    rows, lanes = conv.shape
    x = conv[...].astype(F32)
    extended = jnp.concatenate([rim[...].astype(F32), x], axis=0)
    total = jnp.zeros((rows, lanes), F32)
    for tap in range(CONV):
        start = RIM - (CONV - 1) + tap
        total = total + taps[tap : tap + 1, :] * extended[start : start + rows]
    mixed = (total * jax.nn.sigmoid(total)).astype(BF16)
    mixed_out[...] = mixed
    states = b.shape[1]
    forward = fast_dot(b[...].T, (fade[...] * mixed.astype(F32)).astype(BF16)).astype(BF16)
    first = core[0] == 0
    sent[0:states, :] = jnp.where(first, forward, backward[...])
    kept[0:states, :] = jnp.where(first, backward[...], forward)
    sent[states:, :] = through[...]
    kept[states:, :] = through[...]


def load_kernel(source, held, sem):
    copy = pltpu.make_async_copy(source, held, sem)
    copy.start()
    copy.wait()


def load(source, limit):
    return pl.pallas_call(
        load_kernel,
        out_shape=pltpu.VMEM(source.shape, source.dtype),
        in_specs=[pl.BlockSpec(memory_space=pltpu.HBM)],
        out_specs=pl.BlockSpec(memory_space=pltpu.VMEM),
        scratch_shapes=[pltpu.SemaphoreType.DMA],
        cost_estimate=LIGHT,
        compiler_params=pltpu.CompilerParams(vmem_limit_bytes=limit << 20),
    )(pltpu.with_memory_space_constraint(source, pltpu.HBM))


def after(x, *others):
    return lax.optimization_barrier((x, *others))[0]


def pair_kernel(received, kept, chip):
    states = kept.shape[0] - DECAY_ROWS
    decay = kept[states : states + 1, :].astype(F32)
    got = received[0:states, :].astype(F32)
    chip[0:states, :] = (got * decay + kept[0:states, :].astype(F32)).astype(BF16)
    both = decay * received[states : states + 1, :].astype(F32)
    chip[states:, :] = jnp.broadcast_to(both, (DECAY_ROWS, both.shape[1])).astype(BF16)


def reach_kernel(flip, near, middle, far, mine):
    states = mine.shape[0]
    flipped = flip[0] != 0

    def part(ref):
        return ref[0:states, :].astype(F32), ref[states : states + 1, :].astype(F32)

    a, a_decay = part(near)
    b, b_decay = part(middle)
    c, c_decay = part(far)
    first, first_decay = jnp.where(flipped, c, a), jnp.where(flipped, c_decay, a_decay)
    third = jnp.where(flipped, a, c)
    mine[...] = (first + first_decay * (b + b_decay * third)).astype(BF16)


def inner_kernel(mixed, b, c, decay, grad, skip, out, grad_out):
    heads, rows = decay.shape
    lanes = mixed.shape[1]
    width = lanes // heads
    pack = 128 // width
    columns = decay_columns(decay[...])
    tri_rows = (iota((rows, rows), 0) <= iota((rows, rows), 1)).astype(F32)
    totals = exact_dot(decay[...], tri_rows)
    nt = (((1,), (1,)), ((), ()))
    scores = lax.dot_general(c[...], b[...], nt, preferred_element_type=F32)
    flipped = lax.dot_general(b[...], c[...], nt, preferred_element_type=F32)
    t, s = iota((rows, rows), 0), iota((rows, rows), 1)
    spread = (iota((heads, lanes), 1) // width == iota((heads, lanes), 0)).astype(F32)
    gains = exact_dot(skip[...], spread)
    lane = iota((rows, 128), 1) // width
    for group in range(lanes // 128):
        at = slice(group * 128, group * 128 + 128)
        x = mixed[:, at]
        g = grad[:, at]
        left, right, xs, gs = [], [], [], []
        for k in range(pack):
            h = group * pack + k
            gap = columns[:, h : h + 1] - totals[h : h + 1, :]
            left.append((jnp.exp(jnp.where(t >= s, gap, -1e30)) * scores).astype(BF16))
            right.append((jnp.exp(jnp.where(t <= s, -gap, -1e30)) * flipped).astype(BF16))
            xs.append(jnp.where(lane == k, x, jnp.zeros_like(x)))
            gs.append(jnp.where(lane == k, g, jnp.zeros_like(g)))
        gain = gains[0:1, at]
        out[:, at] = fast_dot(jnp.concatenate(left, 1), jnp.concatenate(xs, 0)) + gain * x.astype(F32)
        grad_out[:, at] = fast_dot(jnp.concatenate(right, 1), jnp.concatenate(gs, 0)) + gain * g.astype(F32)


def choices(ids, mine, masks, rows, chunks):
    named = []
    for mask in range(masks):
        wanted = mine ^ mask
        named.append(((ids[0:1, :] == wanted) | (ids[1:2, :] == wanted)).astype(F32))
    named.append(jnp.zeros((8 - masks, rows), F32))
    names = jnp.concatenate(named, axis=0)
    before, after = iota((rows, rows), 0), iota((rows, rows), 1)
    share = rows // chunks
    tri = ((before <= after) & (before // share == after // share)).astype(BF16)
    return names, fast_dot(names.astype(BF16), tri).astype(jnp.int32)


def choice_kernel(mine, ids, weights, sending, keeping, shares):
    chunks, _, slots, rows = sending.shape
    share = rows // chunks
    chosen = ids[...]
    names, counts = choices(chosen, mine[0], N_MASKS, rows, chunks)
    chunk_of = iota((slots, rows), 1) // share
    slot = iota((slots, rows), 0)
    fills = [counts[m : m + 1, :] - 1 == slot for m in range(N_MASKS)]
    for m in range(N_MASKS):
        row = fills[m] & (names[m : m + 1, :] > 0)
        for chunk in range(chunks):
            sending[chunk, m] = (row & (chunk_of == chunk)).astype(BF16)
    for k in range(TOPK):
        picks = [(fills[m] & (chosen[k : k + 1, :] == mine[0] ^ m)).astype(F32) for m in range(N_MASKS)]
        pick = jnp.concatenate(picks, axis=0).T.astype(BF16)
        for chunk in range(chunks):
            keeping[chunk, k] = pick[chunk * share : (chunk + 1) * share]
    shares[...] = jnp.concatenate([weights[...], jnp.zeros((8 - TOPK, rows), F32)], axis=0).T


def carry_kernel(core, shared, prefix, received, inner, grow, c, sending, *outs):
    own = carried(prefix, received)
    carry = jnp.where(core[0] != 0, own, shared[...].astype(F32))
    out = inner[...] + grow[...] * fast_dot(c[...], carry.astype(BF16))
    out = out.astype(BF16)
    for n, picked in enumerate(outs):
        picked[...] = fast_dot(sending[n // N_MASKS, n % N_MASKS], out).astype(BF16)


def carried(prefix, received):
    states = prefix.shape[0]
    decay = received[states : states + 1, :].astype(F32)
    return prefix[...].astype(F32) * decay + received[0:states, :].astype(F32)


def grad_kernel(core, shared, prefix, received, inner, fade, b, out):
    own = carried(prefix, received)
    carry = jnp.where(core[0] != 0, shared[...].astype(F32), own)
    out[...] = inner[...] + fade[...] * fast_dot(b[...], carry.astype(BF16))


N_MASKS = 4


def norm_kernel(mine, gain, *refs):
    parts, out = refs[:-1], refs[-1]
    width = parts[0].shape[1]
    features = width * len(parts)
    values = [part[...].astype(F32) for part in parts]
    squares = sum(jnp.sum(v * v, axis=1, keepdims=True) for v in values)
    scale = lax.rsqrt(squares / features + EPSILON)
    per_half = len(parts) // 2
    for mask, value in enumerate(values):
        at = mine[0] ^ mask
        to = pl.multiple_of((at % per_half) * width, width)
        gains = gain[:, pl.ds(pl.multiple_of(at * width, width), width)]
        out[at // per_half, :, pl.ds(to, width)] = (value * scale * gains).astype(BF16)


def onward_kernel(along_x, along_y, own, to_x, to_y):
    to_x[0] = along_y[0]
    to_y[0] = along_x[1]
    to_x[1:] = own[...]
    to_y[1:] = own[...]


def join_kernel(from_x, from_y, far):
    far[0] = from_x[0]
    far[1] = from_y[0]


def expert_kernel(n, n_split, *refs):
    blocks, (up, down), outs, (rows_in, hidden) = refs[: 2 * n], refs[2 * n : 2 * n + 2], refs[2 * n + 2 : -2], refs[-2:]
    _, slots, half = blocks[0].shape
    for k, block in enumerate(blocks):
        rows = slice(k * slots, (k + 1) * slots)
        rows_in[rows, :half] = block[0]
        rows_in[rows, half:] = block[1]
    for j in range(0, hidden.shape[1], UP_TILE):
        value = fast_dot(rows_in[...], up[:, j : j + UP_TILE])
        hidden[:, j : j + UP_TILE] = (value * jax.nn.sigmoid(value)).astype(BF16)
    for j in range(0, down.shape[1], DOWN_TILE):
        value = fast_dot(hidden[...], down[:, j : j + DOWN_TILE]).astype(BF16)
        at = slice(j % half, j % half + DOWN_TILE)
        for k in range(2 * n):
            start = (n + k) % (2 * n) * slots
            rows = value[start : start + slots]
            if k < n_split:
                outs[2 * k + j // half][:, at] = rows
            else:
                outs[n_split + k][j // half, :, at] = rows


UP_TILE = 512
DOWN_TILE = 512


def expert_rows(blocks, twins, up, down, n_split=0):
    n = len(blocks)
    _, slots, half = blocks[0].shape
    features, hidden = up.shape
    whole, part = shape_of((2, slots, half), BF16), shape_of((slots, half), BF16)
    outs = call(
        lambda *refs: expert_kernel(n, n_split, *refs),
        [part] * (2 * n_split) + [whole] * (2 * n - n_split),
        scratch=[pltpu.VMEM((2 * n * slots, features), BF16), pltpu.VMEM((2 * n * slots, hidden), BF16)],
        limit=9,
    )(*blocks, *twins, up, down)
    return outs[: n + n_split], outs[n + n_split :]


def both(a, b):
    return (a.astype(F32) + b.astype(F32)).astype(BF16)


def arrive_kernel(from_x, from_y, *refs):
    places, others, (far, along_x, along_y, own, to_x, to_y, rest_x, rest_y) = refs[:3], refs[3:6], refs[6:]
    far[0] = from_x[0]
    far[1] = from_y[0]
    along_x[...] = from_x[1:]
    along_y[...] = from_y[1:]
    to_x[0] = from_y[1]
    to_y[0] = from_x[2]
    direct_sums(places, others, own, to_x.at[1], to_y.at[1], rest_x, rest_y)


def direct_sums(places, others, own, to_x, to_y, rest_x, rest_y):
    here, along_x, along_y = zip(places, others)
    own[...] = both(here[0][...], here[1][...])
    to_x[...] = both(along_x[0][0], along_x[1][0])
    to_y[...] = both(along_y[0][1], along_y[1][1])
    rest_x[...] = both(along_x[0][1], along_x[1][1])
    rest_y[...] = both(along_y[0][0], along_y[1][0])


def middle_kernel(far, far_other, *refs):
    places, others, (own, to_x, to_y, rest_x, rest_y) = refs[:3], refs[3:6], refs[6:]
    to_x[0] = both(far[0], far_other[0])
    to_y[0] = both(far[1], far_other[1])
    direct_sums(places, others, own, to_x.at[1], to_y.at[1], rest_x, rest_y)


def late_kernel(from_x, from_y, rest_x, rest_y, far, first_half, second_half, to_x, to_y):
    to_x[0] = both(rest_x[...], from_y[0])
    to_y[0] = both(rest_y[...], from_x[0])
    to_x[1] = both(far[0], first_half[...])
    to_y[1] = both(far[1], second_half[...])


def relay_kernel(from_x, from_y, rest_x, rest_y, next_x, next_y):
    next_x[...] = both(rest_x[...], from_y[1])
    next_y[...] = both(rest_y[...], from_x[1])


def total_kernel(at_last, mine, own, from_x, from_y, last_x, last_y, *refs):
    outs, total = refs[:-1], refs[-1]
    width = outs[0].shape[1]
    per_half = len(outs) // 2

    def add(a, b, c):
        return (a.astype(F32) + b.astype(F32) + c.astype(F32)).astype(BF16)

    total[0] = add(own[0], from_x[1], last_y[at_last])
    total[1] = add(own[1], last_x[at_last], from_y[1])
    for mask, out in enumerate(outs):
        at = mine[0] ^ mask
        to = pl.multiple_of((at % per_half) * width, width)
        out[...] = total[at // per_half, :, pl.ds(to, width)]


def combine_kernel(chunk, keeping, shares, *refs):
    parts, out = refs[:N_MASKS], refs[-1]
    earlier = refs[N_MASKS:-1]
    share = keeping.shape[2]
    here = slice(chunk * share, (chunk + 1) * share)
    values = jnp.concatenate([part[...] for part in parts], axis=0)
    result = jnp.zeros((share, values.shape[1]), F32)
    for k in range(TOPK):
        result = result + shares[here, k : k + 1] * fast_dot(keeping[chunk, k], values)
    result = result.astype(BF16)
    if earlier:
        out[:share] = earlier[0][...]
        out[share:] = result
    else:
        out[...] = result


def directed(x, mask):
    size = lax.axis_size("ctx")
    route = []
    for i in range(size):
        j = i ^ mask
        if (j > i) == (i % 2 == 1):
            route.append((i, j))
    return lax.ppermute(x, "ctx", route)


def exchange_shards(
    conv_input,
    conv_weight,
    b_proj,
    c_proj,
    log_decay,
    skip_gain,
    grad_in,
    norm_gain,
    expert_ids,
    expert_weights,
    up_weight,
    down_weight,
):
    rows, lanes = conv_input.shape
    heads = log_decay.shape[0]
    states = b_proj.shape[1]
    experts = lax.axis_size("exp")
    features = lanes * experts
    place = lax.axis_index("ctx")
    core = (place & 1).reshape(1)
    chip = place >> 1
    mine = lax.axis_index("exp").reshape(1)
    block = shape_of((rows, lanes), F32)
    payload = shape_of((states + DECAY_ROWS, lanes), BF16)
    slots = 3 * TOPK * rows // (2 * experts * CHUNKS)
    half = features // 2
    row_block = shape_of((2, slots, half), BF16)
    half_block = shape_of((slots, half), BF16)

    flip = jnp.where(place & 1 == 1, chip == 2, chip == 1).astype(jnp.int32).reshape(1)
    edge, core, mine, flip = lax.optimization_barrier((conv_input[rows - RIM :], core, mine, flip))
    rim = passed_along(edge, "ctx", 1)
    params = [
        after(log_decay, edge, core, mine, flip),
        c_proj,
        grad_in,
        b_proj,
        conv_input,
        conv_weight,
        skip_gain.reshape(1, heads),
        norm_gain.reshape(1, features),
        expert_ids.T,
        expert_weights.T,
    ]
    prepared = pl.pallas_call(
        lambda *refs: prepare_kernel(len(params), *refs),
        in_specs=[pl.BlockSpec(memory_space=pltpu.HBM)] * len(params),
        out_specs=[pl.BlockSpec(memory_space=pltpu.VMEM)] * (len(params) + 4),
        out_shape=[pltpu.VMEM(p.shape, p.dtype) for p in params]
        + [block, block, shape_of((states, lanes), BF16), shape_of((DECAY_ROWS, lanes), BF16)],
        scratch_shapes=[pltpu.SemaphoreType.DMA((len(params),))],
        cost_estimate=LIGHT,
        compiler_params=pltpu.CompilerParams(vmem_limit_bytes=6 << 20),
    )(*(pltpu.with_memory_space_constraint(p, pltpu.HBM) for p in params))
    decay, c, grad, b, conv, taps, skip, gain, ids, weights, grow, fade, backward, through = prepared
    mixed, sent, kept = call(
        mix_kernel, [shape_of((rows, lanes), BF16), payload, payload], smem=1
    )(core, conv, rim, taps, b, fade, backward, through)
    received = swap(sent, "ctx", 1)
    chip_sum = call(pair_kernel, payload)(received, kept)
    up = load(after(up_weight[0], chip_sum), 1)
    inner, grad_inner = call(inner_kernel, [block, block])(
        after(mixed, up), b, c, decay, grad, skip
    )
    near, middle, far = (directed(chip_sum, mask) for mask in (2, 4, 6))
    share = rows // CHUNKS
    sending, keeping, shares = call(
        choice_kernel,
        [
            shape_of((CHUNKS, N_MASKS, slots, rows), BF16),
            shape_of((CHUNKS, TOPK, share, N_MASKS * slots), BF16),
            shape_of((rows, 8), F32),
        ],
        smem=1,
    )(mine, after(ids, up, inner), weights)
    prefix = call(reach_kernel, shape_of((states, lanes), BF16), smem=1)(
        after(flip, sending), near, middle, far
    )
    shared = swap(prefix, "ctx", 1)
    picked = call(carry_kernel, [shape_of((slots, lanes), BF16)] * (CHUNKS * experts), smem=1)(
        core, shared, prefix, received, inner, grow, c, sending
    )
    down = load(after(down_weight[0], picked[0]), 1)
    masks = (2, 3, 1)

    def to_experts(chunk):
        parts = picked[chunk * experts : (chunk + 1) * experts]
        arrived = {m: swap(parts[m], "exp", m) for m in masks}
        return [parts[0]] + [arrived[m] for m in range(1, experts)]

    def twin(x):
        return swap(x, "ctx", 1)

    def along(to_x, to_y):
        return swap(to_x, "ctx", 2), swap(to_y, "ctx", 4)

    def results(at_last, *sums):
        return call(
            lambda *refs: total_kernel(at_last, *refs),
            [shape_of((slots, lanes), BF16)] * experts,
            smem=1,
            scratch=[pltpu.VMEM((2, slots, half), BF16)],
        )(mine, *sums)

    def normed(arrived):
        return call(norm_kernel, row_block, smem=1)(mine, gain, *arrived)

    def back(parts):
        arrived = {m: swap(parts[m], "exp", m) for m in masks}
        return [parts[0]] + [arrived[m] for m in range(1, experts)]

    onward = shape_of((3, slots, half), BF16)
    first1, *others1 = to_experts(0)
    own1 = normed([after(first1, down), *others1])
    x1, y1 = along(own1, own1)
    arrived2 = to_experts(1)
    own2 = normed(arrived2)
    twin_own1 = twin(after(own1, arrived2[1]))
    to_x, to_y = call(onward_kernel, [onward, onward])(x1, y1, after(own2, twin_own1))
    from_x, from_y = along(to_x, to_y)
    double = shape_of((2, slots, half), BF16)
    sums = [row_block, double, double, half_block, half_block]
    now = [own1, after(x1, to_x), after(y1, to_x), own2]
    twins = [twin_own1] + [twin(block) for block in now[1:]]
    (*odd1, odd_own2), (*even1, even_own2) = expert_rows(now, twins, up, down)
    far1, x2, y2, own_sum1, to_x, to_y, rest_x1, rest_y1 = call(arrive_kernel, [row_block] * 3 + sums)(
        after(from_x, even1[0]), from_y, *even1, *(twin(block) for block in odd1)
    )
    from_x3, from_y3 = along(to_x, to_y)
    now = [far1, x2, y2]
    odd, even = expert_rows(now, [twin(block) for block in now], up, down)
    far2 = call(join_kernel, row_block)(after(from_x3, even[0]), from_y3)
    own_sum2, to_x, to_y, rest_x2, rest_y2 = call(middle_kernel, sums)(
        after(even[0], far2), twin(odd[0]),
        even_own2, *even[1:], twin(odd_own2), *(twin(block) for block in odd[1:]),
    )
    from_x4, from_y4 = along(to_x, to_y)
    odd_far2, (even_far2,) = expert_rows(
        [after(far2, own_sum2)], [twin(far2)], up, down, n_split=1
    )
    to_x, to_y = call(late_kernel, [double, double])(
        from_x4, from_y4, rest_x1, rest_y1, even_far2, *(twin(part) for part in odd_far2)
    )
    from_x5, from_y5 = along(to_x, to_y)
    grad_conv = call(grad_kernel, block, smem=1)(
        core, shared, after(prefix, to_x), received, grad_inner, fade, b
    )
    next_x, next_y = call(relay_kernel, [half_block, half_block])(from_x5, from_y5, after(rest_x2, grad_conv), rest_y2)
    done1 = results(0, own_sum1, from_x3, from_y3, after(from_x5, next_x), from_y5)
    last_x, last_y = along(next_x, next_y)
    back1 = back(done1)
    done2 = results(slice(None), own_sum2, from_x4, from_y4, last_x, last_y)
    combined = call(lambda *refs: combine_kernel(0, *refs), shape_of((share, lanes), BF16))(
        after(keeping, done2[0]), shares, *back1
    )
    moe_out = call(lambda *refs: combine_kernel(1, *refs), shape_of((rows, lanes), BF16))(
        keeping, shares, *back(done2), combined
    )
    return (moe_out, grad_conv)


def solution(mesh):
    placed = (
        P("ctx", "exp"),
        P(None, "exp"),
        P("ctx", None),
        P("ctx", None),
        P("exp", "ctx"),
        P("exp"),
        P("ctx", "exp"),
        P(),
        P("ctx", None),
        P("ctx", None),
        P("exp", None, "ctx"),
        P("exp", "ctx", None),
    )
    swaps = mesh.shape["ctx"] == 8 and mesh.shape["exp"] == 4
    return jax.shard_map(
        exchange_shards if swaps else general_shards,
        mesh=mesh,
        in_specs=placed,
        out_specs=(P("ctx", "exp"), P("ctx", "exp")),
        check_vma=False,
    )
```

```python
import jax
import jax.numpy as jnp
from jax import lax
from jax.experimental import pallas as pl
from jax.experimental.pallas import tpu as pltpu
from jax.sharding import PartitionSpec as P

CONV = 4
TOPK = 2


HIGHEST = lax.Precision.HIGHEST
EPSILON = 1e-06


def passed_along(block, axis, distance):
    devices = range(lax.axis_size(axis))
    route = [(i - distance, i) for i in devices if i - distance in devices]
    return lax.ppermute(block, axis, route)


def prefix(x, axis, combine, identity, reverse):
    size, mine = (lax.axis_size(axis), lax.axis_index(axis))
    everything = jax.tree.map(
        lambda part, kind: lax.all_gather(part.astype(kind), axis), x, (jnp.bfloat16, jnp.bfloat16)
    )
    start = jax.tree.map(
        lambda part, zero: jnp.broadcast_to(jnp.asarray(zero, part.dtype), part.shape), x, identity
    )

    def turn(k, before):
        at = size - 1 - k if reverse else k
        reached = at > mine if reverse else at < mine
        new = combine(
            before, jax.tree.map(lambda part, own: part[at].astype(own.dtype), everything, x)
        )
        return jax.tree.map(lambda a, b: jnp.where(reached, a, b), new, before)

    return lax.fori_loop(0, size, turn, start)


def combine_state(earlier, later):
    return (earlier[0] * later[0], later[0][:, None, None] * earlier[1] + later[1])


def conv_mix(extended, conv_weight):
    rows_out = extended.shape[0] - conv_weight.shape[0] + 1
    total = jnp.zeros((rows_out, extended.shape[1]), jnp.float32)
    for offset in range(conv_weight.shape[0]):
        total = total + conv_weight[offset][None, :] * extended[offset : offset + rows_out]
    return jax.nn.silu(total).astype(jnp.bfloat16)


def block_terms(decay_block, b_raw, c_raw):
    totals = jnp.cumsum(decay_block, axis=1)
    rows_here = totals.shape[1]
    causal = jnp.arange(rows_here)[:, None] >= jnp.arange(rows_here)[None, :]
    spread = jnp.where(causal[None], totals[:, :, None] - totals[:, None, :], 0.0)
    kernel = (
        jnp.where(causal[None], jnp.exp(spread), 0.0)
        * jnp.dot(c_raw, b_raw.T, preferred_element_type=jnp.float32)[None]
    )
    to_end = jnp.exp(totals[:, -1:] - totals)
    return (totals, kernel, to_end)


def normalize(rows_in, norm_gain):
    values = rows_in.astype(jnp.float32)
    scale = lax.rsqrt(jnp.mean(values * values, axis=1, keepdims=True) + EPSILON)
    return (values * scale * norm_gain[None, :]).astype(jnp.bfloat16)


def route_matrix(chosen_ids, slots_each, experts):
    pairs = chosen_ids.reshape(-1)
    onehot = (pairs[:, None] == jnp.arange(experts, dtype=jnp.int32)[None, :]).astype(jnp.int32)
    ranks = jnp.sum((jnp.cumsum(onehot, axis=0) - 1) * onehot, axis=1)
    target = pairs * slots_each + ranks
    return (jnp.arange(experts * slots_each, dtype=jnp.int32)[:, None] == target[None, :]).astype(
        jnp.bfloat16
    )


def gather_back(dispatch, returned, weights):
    values = jnp.einsum("sp,sc->pc", dispatch, returned, preferred_element_type=jnp.float32)
    values = values.reshape(weights.shape[0], weights.shape[1], returned.shape[1])
    return jnp.sum(weights[:, :, None] * values, axis=1).astype(jnp.bfloat16)


def expert_block(rows_in, up_weight, down_weight):
    up_local = up_weight[0]
    down_local = down_weight[0]
    hidden = jax.nn.silu(
        jnp.dot(
            lax.all_gather(rows_in, "ctx", axis=0, tiled=True),
            up_local,
            preferred_element_type=jnp.float32,
        )
    ).astype(jnp.bfloat16)
    summed = lax.psum_scatter(
        jnp.dot(hidden, down_local, preferred_element_type=jnp.float32).astype(jnp.bfloat16),
        "ctx",
        scatter_dimension=0,
        tiled=True,
    )
    return summed


def general_shards(
    conv_input,
    conv_weight,
    b_proj,
    c_proj,
    log_decay,
    skip_gain,
    grad_in,
    norm_gain,
    expert_ids,
    expert_weights,
    up_weight,
    down_weight,
):
    tok_rows = conv_input.shape[0]
    heads_here = log_decay.shape[0]
    head_size = conv_input.shape[1] // heads_here
    rim_rows = passed_along(conv_input[tok_rows - (CONV - 1) :], "ctx", 1)
    extended = jnp.concatenate(
        [rim_rows.astype(jnp.float32), conv_input.astype(jnp.float32)], axis=0
    )
    mixed_in = conv_mix(extended, conv_weight)
    inputs_block = mixed_in.astype(jnp.float32).reshape(tok_rows, heads_here, head_size)
    b_block = b_proj.astype(jnp.float32)
    c_block = c_proj.astype(jnp.float32)
    grad_block = grad_in.astype(jnp.float32).reshape(tok_rows, heads_here, head_size)
    totals, kernel, to_end = block_terms(log_decay, b_proj, c_proj)
    through = jnp.exp(totals[:, -1])
    local_state = jnp.einsum("hs,shp,sn->hpn", to_end, inputs_block, b_block, precision=HIGHEST)
    local_grad = jnp.einsum(
        "ht,thp,tn->hpn", jnp.exp(totals), grad_block, c_block, precision=HIGHEST
    )
    zero_state = jnp.zeros_like(local_state)
    ones_heads = jnp.ones_like(through)
    carry_state = prefix(
        (through, local_state), "ctx", combine_state, (ones_heads, zero_state), False
    )[1]
    carry_grad = prefix(
        (through, local_grad), "ctx", combine_state, (ones_heads, zero_state), True
    )[1]
    inner = jnp.einsum("hts,shp->thp", kernel, inputs_block, precision=HIGHEST)
    carried = jnp.exp(totals).T[:, :, None] * jnp.einsum(
        "hpn,tn->thp", carry_state, c_block, precision=HIGHEST
    )
    output = inner + carried + skip_gain[None, :, None] * inputs_block
    ssd_out = output.reshape(tok_rows, heads_here * head_size).astype(jnp.bfloat16)
    grad_inner = jnp.einsum("hts,thp->shp", kernel, grad_block, precision=HIGHEST)
    grad_carried = to_end.T[:, :, None] * jnp.einsum(
        "hpn,sn->shp", carry_grad, b_block, precision=HIGHEST
    )
    grad_conv = (grad_inner + grad_carried + skip_gain[None, :, None] * grad_block).reshape(
        tok_rows, heads_here * head_size
    )
    experts = lax.axis_size("exp")
    most_rows = 3 * TOPK * tok_rows // (2 * experts * experts)
    share = tok_rows // experts
    token_view = lax.all_to_all(ssd_out, "exp", split_axis=0, concat_axis=1, tiled=True)
    normed = normalize(token_view, norm_gain)
    first_row = lax.axis_index("exp") * share
    my_ids = lax.dynamic_slice_in_dim(expert_ids, first_row, share, 0)
    my_weights = lax.dynamic_slice_in_dim(expert_weights, first_row, share, 0)
    dispatch = route_matrix(my_ids, most_rows, experts)
    outgoing = jnp.dot(
        dispatch, jnp.repeat(normed, TOPK, axis=0), preferred_element_type=jnp.float32
    ).astype(jnp.bfloat16)
    incoming = lax.all_to_all(
        outgoing.reshape(experts, most_rows, normed.shape[1]),
        "exp",
        split_axis=0,
        concat_axis=0,
        tiled=True,
    )
    results = expert_block(
        incoming.reshape(experts * most_rows, normed.shape[1]), up_weight, down_weight
    )
    returned = lax.all_to_all(
        results.reshape(experts, most_rows, normed.shape[1]),
        "exp",
        split_axis=0,
        concat_axis=0,
        tiled=True,
    )
    combined = gather_back(
        dispatch, returned.reshape(experts * most_rows, normed.shape[1]), my_weights
    )
    moe_out = lax.all_to_all(combined, "exp", split_axis=1, concat_axis=0, tiled=True)
    return (moe_out, grad_conv)


CHUNKS = 2
LIGHT = pl.CostEstimate(flops=1, transcendentals=0, bytes_accessed=1)
DECAY_ROWS = 8
RIM = 8
F32 = jnp.float32
BF16 = jnp.bfloat16


def shape_of(shape, dtype):
    return jax.ShapeDtypeStruct(shape, dtype)


def call(body, outs, smem=0, scratch=(), limit=6):
    def run(*args):
        specs = [pl.BlockSpec(memory_space=pltpu.SMEM)] * smem
        specs += [pl.BlockSpec(memory_space=pltpu.VMEM)] * (len(args) - smem)
        return pl.pallas_call(
            body,
            out_shape=outs,
            in_specs=specs,
            out_specs=jax.tree.map(lambda _: pl.BlockSpec(memory_space=pltpu.VMEM), outs),
            scratch_shapes=scratch,
            cost_estimate=LIGHT,
            compiler_params=pltpu.CompilerParams(vmem_limit_bytes=limit << 20),
        )(*args)

    return run


def swap(x, axis, mask):
    size = lax.axis_size(axis)
    return lax.ppermute(x, axis, [(i, i ^ mask) for i in range(size)])


def exact_dot(a, b, dims=(((1,), (0,)), ((), ()))):
    return lax.dot_general(a, b, dims, precision=HIGHEST, preferred_element_type=F32)


def fast_dot(a, b):
    return jnp.dot(a, b, preferred_element_type=F32)


def iota(shape, dim):
    return lax.broadcasted_iota(jnp.int32, shape, dim)


def decay_columns(decay):
    rows = decay.shape[1]
    tri = (iota((rows, rows), 0) >= iota((rows, rows), 1)).astype(F32)
    return exact_dot(tri, decay, (((1,), (1,)), ((), ())))


def prepare_kernel(n, *refs):
    sources, held = refs[:n], refs[n : 2 * n]
    grow, fade, backward, through, sems = refs[2 * n :]
    copies = [pltpu.make_async_copy(a, b, sems.at[k]) for k, (a, b) in enumerate(zip(sources, held))]
    for copy in copies:
        copy.start()
    for copy in copies:
        copy.wait()
    decay, c, grad = held[:3]
    heads = decay.shape[0]
    rows, lanes = grad.shape
    columns = decay_columns(decay[...])
    width = lanes // heads
    spread = (iota((heads, lanes), 1) // width == iota((heads, lanes), 0)).astype(F32)
    totals = exact_dot(columns, spread)
    last = totals[rows - 1 : rows, :]
    growing = jnp.exp(totals)
    grow[...] = growing
    fade[...] = jnp.exp(last - totals)
    through[...] = jnp.broadcast_to(jnp.exp(last), (DECAY_ROWS, lanes)).astype(BF16)
    backward[...] = fast_dot(c[...].T, (growing * grad[...].astype(F32)).astype(BF16)).astype(BF16)


def mix_kernel(core, conv, rim, taps, b, fade, backward, through, mixed_out, sent, kept):
    rows, lanes = conv.shape
    x = conv[...].astype(F32)
    extended = jnp.concatenate([rim[...].astype(F32), x], axis=0)
    total = jnp.zeros((rows, lanes), F32)
    for tap in range(CONV):
        start = RIM - (CONV - 1) + tap
        total = total + taps[tap : tap + 1, :] * extended[start : start + rows]
    mixed = (total * jax.nn.sigmoid(total)).astype(BF16)
    mixed_out[...] = mixed
    states = b.shape[1]
    forward = fast_dot(b[...].T, (fade[...] * mixed.astype(F32)).astype(BF16)).astype(BF16)
    first = core[0] == 0
    sent[0:states, :] = jnp.where(first, forward, backward[...])
    kept[0:states, :] = jnp.where(first, backward[...], forward)
    sent[states:, :] = through[...]
    kept[states:, :] = through[...]


def load_kernel(source, held, sem):
    copy = pltpu.make_async_copy(source, held, sem)
    copy.start()
    copy.wait()


def load(source, limit):
    return pl.pallas_call(
        load_kernel,
        out_shape=pltpu.VMEM(source.shape, source.dtype),
        in_specs=[pl.BlockSpec(memory_space=pltpu.HBM)],
        out_specs=pl.BlockSpec(memory_space=pltpu.VMEM),
        scratch_shapes=[pltpu.SemaphoreType.DMA],
        cost_estimate=LIGHT,
        compiler_params=pltpu.CompilerParams(vmem_limit_bytes=limit << 20),
    )(pltpu.with_memory_space_constraint(source, pltpu.HBM))


def after(x, *others):
    return lax.optimization_barrier((x, *others))[0]


def pair_kernel(received, kept, chip):
    states = kept.shape[0] - DECAY_ROWS
    decay = kept[states : states + 1, :].astype(F32)
    got = received[0:states, :].astype(F32)
    chip[0:states, :] = (got * decay + kept[0:states, :].astype(F32)).astype(BF16)
    both = decay * received[states : states + 1, :].astype(F32)
    chip[states:, :] = jnp.broadcast_to(both, (DECAY_ROWS, both.shape[1])).astype(BF16)


def reach_kernel(flip, near, middle, far, mine):
    states = mine.shape[0]
    flipped = flip[0] != 0

    def part(ref):
        return ref[0:states, :].astype(F32), ref[states : states + 1, :].astype(F32)

    a, a_decay = part(near)
    b, b_decay = part(middle)
    c, c_decay = part(far)
    first, first_decay = jnp.where(flipped, c, a), jnp.where(flipped, c_decay, a_decay)
    third = jnp.where(flipped, a, c)
    mine[...] = (first + first_decay * (b + b_decay * third)).astype(BF16)


def inner_kernel(mixed, b, c, decay, grad, skip, out, grad_out):
    heads, rows = decay.shape
    lanes = mixed.shape[1]
    width = lanes // heads
    pack = 128 // width
    columns = decay_columns(decay[...])
    tri_rows = (iota((rows, rows), 0) <= iota((rows, rows), 1)).astype(F32)
    totals = exact_dot(decay[...], tri_rows)
    nt = (((1,), (1,)), ((), ()))
    scores = lax.dot_general(c[...], b[...], nt, preferred_element_type=F32)
    flipped = lax.dot_general(b[...], c[...], nt, preferred_element_type=F32)
    t, s = iota((rows, rows), 0), iota((rows, rows), 1)
    spread = (iota((heads, lanes), 1) // width == iota((heads, lanes), 0)).astype(F32)
    gains = exact_dot(skip[...], spread)
    lane = iota((rows, 128), 1) // width
    for group in range(lanes // 128):
        at = slice(group * 128, group * 128 + 128)
        x = mixed[:, at]
        g = grad[:, at]
        left, right, xs, gs = [], [], [], []
        for k in range(pack):
            h = group * pack + k
            gap = columns[:, h : h + 1] - totals[h : h + 1, :]
            left.append((jnp.exp(jnp.where(t >= s, gap, -1e30)) * scores).astype(BF16))
            right.append((jnp.exp(jnp.where(t <= s, -gap, -1e30)) * flipped).astype(BF16))
            xs.append(jnp.where(lane == k, x, jnp.zeros_like(x)))
            gs.append(jnp.where(lane == k, g, jnp.zeros_like(g)))
        gain = gains[0:1, at]
        out[:, at] = fast_dot(jnp.concatenate(left, 1), jnp.concatenate(xs, 0)) + gain * x.astype(F32)
        grad_out[:, at] = fast_dot(jnp.concatenate(right, 1), jnp.concatenate(gs, 0)) + gain * g.astype(F32)


def choices(ids, mine, masks, rows, chunks):
    named = []
    for mask in range(masks):
        wanted = mine ^ mask
        named.append(((ids[0:1, :] == wanted) | (ids[1:2, :] == wanted)).astype(F32))
    named.append(jnp.zeros((8 - masks, rows), F32))
    names = jnp.concatenate(named, axis=0)
    before, after = iota((rows, rows), 0), iota((rows, rows), 1)
    share = rows // chunks
    tri = ((before <= after) & (before // share == after // share)).astype(BF16)
    return names, fast_dot(names.astype(BF16), tri).astype(jnp.int32)


def choice_kernel(mine, ids, weights, sending, keeping, shares):
    chunks, _, slots, rows = sending.shape
    share = rows // chunks
    chosen = ids[...]
    names, counts = choices(chosen, mine[0], N_MASKS, rows, chunks)
    chunk_of = iota((slots, rows), 1) // share
    slot = iota((slots, rows), 0)
    fills = [counts[m : m + 1, :] - 1 == slot for m in range(N_MASKS)]
    for m in range(N_MASKS):
        row = fills[m] & (names[m : m + 1, :] > 0)
        for chunk in range(chunks):
            sending[chunk, m] = (row & (chunk_of == chunk)).astype(BF16)
    for k in range(TOPK):
        picks = [(fills[m] & (chosen[k : k + 1, :] == mine[0] ^ m)).astype(F32) for m in range(N_MASKS)]
        pick = jnp.concatenate(picks, axis=0).T.astype(BF16)
        for chunk in range(chunks):
            keeping[chunk, k] = pick[chunk * share : (chunk + 1) * share]
    shares[...] = jnp.concatenate([weights[...], jnp.zeros((8 - TOPK, rows), F32)], axis=0).T


def carry_kernel(core, shared, prefix, received, inner, grow, c, sending, *outs):
    own = carried(prefix, received)
    carry = jnp.where(core[0] != 0, own, shared[...].astype(F32))
    out = inner[...] + grow[...] * fast_dot(c[...], carry.astype(BF16))
    out = out.astype(BF16)
    for n, picked in enumerate(outs):
        picked[...] = fast_dot(sending[n // N_MASKS, n % N_MASKS], out).astype(BF16)


def carried(prefix, received):
    states = prefix.shape[0]
    decay = received[states : states + 1, :].astype(F32)
    return prefix[...].astype(F32) * decay + received[0:states, :].astype(F32)


def grad_kernel(core, shared, prefix, received, inner, fade, b, out):
    own = carried(prefix, received)
    carry = jnp.where(core[0] != 0, shared[...].astype(F32), own)
    out[...] = inner[...] + fade[...] * fast_dot(b[...], carry.astype(BF16))


N_MASKS = 4


def norm_kernel(mine, gain, *refs):
    parts, out = refs[:-1], refs[-1]
    width = parts[0].shape[1]
    features = width * len(parts)
    values = [part[...].astype(F32) for part in parts]
    squares = sum(jnp.sum(v * v, axis=1, keepdims=True) for v in values)
    scale = lax.rsqrt(squares / features + EPSILON)
    per_half = len(parts) // 2
    for mask, value in enumerate(values):
        at = mine[0] ^ mask
        to = pl.multiple_of((at % per_half) * width, width)
        gains = gain[:, pl.ds(pl.multiple_of(at * width, width), width)]
        out[at // per_half, :, pl.ds(to, width)] = (value * scale * gains).astype(BF16)


def onward_kernel(along_x, along_y, own, to_x, to_y):
    to_x[0] = along_y[0]
    to_y[0] = along_x[1]
    to_x[1:] = own[...]
    to_y[1:] = own[...]


def join_kernel(from_x, from_y, far):
    far[0] = from_x[0]
    far[1] = from_y[0]


def expert_kernel(n, n_split, *refs):
    blocks, (up, down), outs, (rows_in, hidden) = refs[: 2 * n], refs[2 * n : 2 * n + 2], refs[2 * n + 2 : -2], refs[-2:]
    _, slots, half = blocks[0].shape
    for k, block in enumerate(blocks):
        rows = slice(k * slots, (k + 1) * slots)
        rows_in[rows, :half] = block[0]
        rows_in[rows, half:] = block[1]
    for j in range(0, hidden.shape[1], UP_TILE):
        value = fast_dot(rows_in[...], up[:, j : j + UP_TILE])
        hidden[:, j : j + UP_TILE] = (value * jax.nn.sigmoid(value)).astype(BF16)
    for j in range(0, down.shape[1], DOWN_TILE):
        value = fast_dot(hidden[...], down[:, j : j + DOWN_TILE]).astype(BF16)
        at = slice(j % half, j % half + DOWN_TILE)
        for k in range(2 * n):
            start = (n + k) % (2 * n) * slots
            rows = value[start : start + slots]
            if k < n_split:
                outs[2 * k + j // half][:, at] = rows
            else:
                outs[n_split + k][j // half, :, at] = rows


UP_TILE = 512
DOWN_TILE = 512


def expert_rows(blocks, twins, up, down, n_split=0):
    n = len(blocks)
    _, slots, half = blocks[0].shape
    features, hidden = up.shape
    whole, part = shape_of((2, slots, half), BF16), shape_of((slots, half), BF16)
    outs = call(
        lambda *refs: expert_kernel(n, n_split, *refs),
        [part] * (2 * n_split) + [whole] * (2 * n - n_split),
        scratch=[pltpu.VMEM((2 * n * slots, features), BF16), pltpu.VMEM((2 * n * slots, hidden), BF16)],
        limit=9,
    )(*blocks, *twins, up, down)
    return outs[: n + n_split], outs[n + n_split :]


def both(a, b):
    return (a.astype(F32) + b.astype(F32)).astype(BF16)


def arrive_kernel(from_x, from_y, *refs):
    places, others, (far, along_x, along_y, own, to_x, to_y, rest_x, rest_y) = refs[:3], refs[3:6], refs[6:]
    far[0] = from_x[0]
    far[1] = from_y[0]
    along_x[...] = from_x[1:]
    along_y[...] = from_y[1:]
    to_x[0] = from_y[1]
    to_y[0] = from_x[2]
    direct_sums(places, others, own, to_x.at[1], to_y.at[1], rest_x, rest_y)


def direct_sums(places, others, own, to_x, to_y, rest_x, rest_y):
    here, along_x, along_y = zip(places, others)
    own[...] = both(here[0][...], here[1][...])
    to_x[...] = both(along_x[0][0], along_x[1][0])
    to_y[...] = both(along_y[0][1], along_y[1][1])
    rest_x[...] = both(along_x[0][1], along_x[1][1])
    rest_y[...] = both(along_y[0][0], along_y[1][0])


def middle_kernel(far, far_other, *refs):
    places, others, (own, to_x, to_y, rest_x, rest_y) = refs[:3], refs[3:6], refs[6:]
    to_x[0] = both(far[0], far_other[0])
    to_y[0] = both(far[1], far_other[1])
    direct_sums(places, others, own, to_x.at[1], to_y.at[1], rest_x, rest_y)


def late_kernel(from_x, from_y, rest_x, rest_y, far, first_half, second_half, to_x, to_y):
    to_x[0] = both(rest_x[...], from_y[0])
    to_y[0] = both(rest_y[...], from_x[0])
    to_x[1] = both(far[0], first_half[...])
    to_y[1] = both(far[1], second_half[...])


def relay_kernel(from_x, from_y, rest_x, rest_y, next_x, next_y):
    next_x[...] = both(rest_x[...], from_y[1])
    next_y[...] = both(rest_y[...], from_x[1])


def total_kernel(at_last, mine, own, from_x, from_y, last_x, last_y, *refs):
    outs, total = refs[:-1], refs[-1]
    width = outs[0].shape[1]
    per_half = len(outs) // 2

    def add(a, b, c):
        return (a.astype(F32) + b.astype(F32) + c.astype(F32)).astype(BF16)

    total[0] = add(own[0], from_x[1], last_y[at_last])
    total[1] = add(own[1], last_x[at_last], from_y[1])
    for mask, out in enumerate(outs):
        at = mine[0] ^ mask
        to = pl.multiple_of((at % per_half) * width, width)
        out[...] = total[at // per_half, :, pl.ds(to, width)]


def combine_kernel(chunk, keeping, shares, *refs):
    parts, out = refs[:N_MASKS], refs[-1]
    earlier = refs[N_MASKS:-1]
    share = keeping.shape[2]
    here = slice(chunk * share, (chunk + 1) * share)
    values = jnp.concatenate([part[...] for part in parts], axis=0)
    result = jnp.zeros((share, values.shape[1]), F32)
    for k in range(TOPK):
        result = result + shares[here, k : k + 1] * fast_dot(keeping[chunk, k], values)
    result = result.astype(BF16)
    if earlier:
        out[:share] = earlier[0][...]
        out[share:] = result
    else:
        out[...] = result


def directed(x, mask):
    size = lax.axis_size("ctx")
    route = []
    for i in range(size):
        j = i ^ mask
        if (j > i) == (i % 2 == 1):
            route.append((i, j))
    return lax.ppermute(x, "ctx", route)


def exchange_shards(
    conv_input,
    conv_weight,
    b_proj,
    c_proj,
    log_decay,
    skip_gain,
    grad_in,
    norm_gain,
    expert_ids,
    expert_weights,
    up_weight,
    down_weight,
):
    rows, lanes = conv_input.shape
    heads = log_decay.shape[0]
    states = b_proj.shape[1]
    experts = lax.axis_size("exp")
    features = lanes * experts
    place = lax.axis_index("ctx")
    core = (place & 1).reshape(1)
    chip = place >> 1
    mine = lax.axis_index("exp").reshape(1)
    block = shape_of((rows, lanes), F32)
    payload = shape_of((states + DECAY_ROWS, lanes), BF16)
    slots = 3 * TOPK * rows // (2 * experts * CHUNKS)
    half = features // 2
    row_block = shape_of((2, slots, half), BF16)
    half_block = shape_of((slots, half), BF16)

    flip = jnp.where(place & 1 == 1, chip == 2, chip == 1).astype(jnp.int32).reshape(1)
    edge, core, mine, flip = lax.optimization_barrier((conv_input[rows - RIM :], core, mine, flip))
    rim = passed_along(edge, "ctx", 1)
    params = [
        after(log_decay, edge, core, mine, flip),
        c_proj,
        grad_in,
        b_proj,
        conv_input,
        conv_weight,
        skip_gain.reshape(1, heads),
        norm_gain.reshape(1, features),
        expert_ids.T,
        expert_weights.T,
    ]
    prepared = pl.pallas_call(
        lambda *refs: prepare_kernel(len(params), *refs),
        in_specs=[pl.BlockSpec(memory_space=pltpu.HBM)] * len(params),
        out_specs=[pl.BlockSpec(memory_space=pltpu.VMEM)] * (len(params) + 4),
        out_shape=[pltpu.VMEM(p.shape, p.dtype) for p in params]
        + [block, block, shape_of((states, lanes), BF16), shape_of((DECAY_ROWS, lanes), BF16)],
        scratch_shapes=[pltpu.SemaphoreType.DMA((len(params),))],
        cost_estimate=LIGHT,
        compiler_params=pltpu.CompilerParams(vmem_limit_bytes=6 << 20),
    )(*(pltpu.with_memory_space_constraint(p, pltpu.HBM) for p in params))
    decay, c, grad, b, conv, taps, skip, gain, ids, weights, grow, fade, backward, through = prepared
    mixed, sent, kept = call(
        mix_kernel, [shape_of((rows, lanes), BF16), payload, payload], smem=1
    )(core, conv, rim, taps, b, fade, backward, through)
    received = swap(sent, "ctx", 1)
    chip_sum = call(pair_kernel, payload)(received, kept)
    up = load(after(up_weight[0], chip_sum), 1)
    inner, grad_inner = call(inner_kernel, [block, block])(
        after(mixed, up), b, c, decay, grad, skip
    )
    near, middle, far = (directed(chip_sum, mask) for mask in (2, 4, 6))
    share = rows // CHUNKS
    sending, keeping, shares = call(
        choice_kernel,
        [
            shape_of((CHUNKS, N_MASKS, slots, rows), BF16),
            shape_of((CHUNKS, TOPK, share, N_MASKS * slots), BF16),
            shape_of((rows, 8), F32),
        ],
        smem=1,
    )(mine, after(ids, up, inner), weights)
    prefix = call(reach_kernel, shape_of((states, lanes), BF16), smem=1)(
        after(flip, sending), near, middle, far
    )
    shared = swap(prefix, "ctx", 1)
    picked = call(carry_kernel, [shape_of((slots, lanes), BF16)] * (CHUNKS * experts), smem=1)(
        core, shared, prefix, received, inner, grow, c, sending
    )
    down = load(after(down_weight[0], picked[0]), 1)
    masks = (3, 2, 1)

    def to_experts(chunk):
        parts = picked[chunk * experts : (chunk + 1) * experts]
        arrived = {m: swap(parts[m], "exp", m) for m in masks}
        return [parts[0]] + [arrived[m] for m in range(1, experts)]

    def twin(x):
        return swap(x, "ctx", 1)

    def along(to_x, to_y):
        return swap(to_x, "ctx", 2), swap(to_y, "ctx", 4)

    def results(at_last, *sums):
        return call(
            lambda *refs: total_kernel(at_last, *refs),
            [shape_of((slots, lanes), BF16)] * experts,
            smem=1,
            scratch=[pltpu.VMEM((2, slots, half), BF16)],
        )(mine, *sums)

    def normed(arrived):
        return call(norm_kernel, row_block, smem=1)(mine, gain, *arrived)

    def back(parts):
        arrived = {m: swap(parts[m], "exp", m) for m in masks}
        return [parts[0]] + [arrived[m] for m in range(1, experts)]

    onward = shape_of((3, slots, half), BF16)
    first1, *others1 = to_experts(0)
    own1 = normed([after(first1, down), *others1])
    x1, y1 = along(own1, own1)
    arrived2 = to_experts(1)
    own2 = normed(arrived2)
    twin_own1 = twin(after(own1, arrived2[1]))
    to_x, to_y = call(onward_kernel, [onward, onward])(x1, y1, after(own2, twin_own1))
    from_x, from_y = along(to_x, to_y)
    double = shape_of((2, slots, half), BF16)
    sums = [row_block, double, double, half_block, half_block]
    now = [own1, after(x1, to_x), after(y1, to_x), own2]
    twins = [twin_own1] + [twin(block) for block in now[1:]]
    (*odd1, odd_own2), (*even1, even_own2) = expert_rows(now, twins, up, down)
    far1, x2, y2, own_sum1, to_x, to_y, rest_x1, rest_y1 = call(arrive_kernel, [row_block] * 3 + sums)(
        after(from_x, even1[0]), from_y, *even1, *(twin(block) for block in odd1)
    )
    from_x3, from_y3 = along(to_x, to_y)
    now = [far1, x2, y2]
    odd, even = expert_rows(now, [twin(block) for block in now], up, down)
    far2 = call(join_kernel, row_block)(after(from_x3, even[0]), from_y3)
    own_sum2, to_x, to_y, rest_x2, rest_y2 = call(middle_kernel, sums)(
        after(even[0], far2), twin(odd[0]),
        even_own2, *even[1:], twin(odd_own2), *(twin(block) for block in odd[1:]),
    )
    from_x4, from_y4 = along(to_x, to_y)
    odd_far2, (even_far2,) = expert_rows(
        [after(far2, own_sum2)], [twin(far2)], up, down, n_split=1
    )
    to_x, to_y = call(late_kernel, [double, double])(
        from_x4, from_y4, rest_x1, rest_y1, even_far2, *(twin(part) for part in odd_far2)
    )
    from_x5, from_y5 = along(to_x, to_y)
    grad_conv = call(grad_kernel, block, smem=1)(
        core, shared, after(prefix, to_x), received, grad_inner, fade, b
    )
    next_x, next_y = call(relay_kernel, [half_block, half_block])(from_x5, from_y5, after(rest_x2, grad_conv), rest_y2)
    done1 = results(0, own_sum1, from_x3, from_y3, after(from_x5, next_x), from_y5)
    last_x, last_y = along(next_x, next_y)
    back1 = back(done1)
    done2 = results(slice(None), own_sum2, from_x4, from_y4, last_x, last_y)
    combined = call(lambda *refs: combine_kernel(0, *refs), shape_of((share, lanes), BF16))(
        after(keeping, done2[0]), shares, *back1
    )
    moe_out = call(lambda *refs: combine_kernel(1, *refs), shape_of((rows, lanes), BF16))(
        keeping, shares, *back(done2), combined
    )
    return (moe_out, grad_conv)


def solution(mesh):
    placed = (
        P("ctx", "exp"),
        P(None, "exp"),
        P("ctx", None),
        P("ctx", None),
        P("exp", "ctx"),
        P("exp"),
        P("ctx", "exp"),
        P(),
        P("ctx", None),
        P("ctx", None),
        P("exp", None, "ctx"),
        P("exp", "ctx", None),
    )
    swaps = mesh.shape["ctx"] == 8 and mesh.shape["exp"] == 4
    return jax.shard_map(
        exchange_shards if swaps else general_shards,
        mesh=mesh,
        in_specs=placed,
        out_specs=(P("ctx", "exp"), P("ctx", "exp")),
        check_vma=False,
    )
```
